256 devices in a mesh: tile: 64 (over z, y, core), cuts: 4 (over x).
Axes of the slice: x: 4, y: 4, z: 8, core: 2. Of those that a mesh axis runs over, the one named last changes fastest.
Arguments:
- transmission: float32 [4, 2, 16384, 1024], P('cuts', None, 'tile')
- probe: float32 [2, 256, 256], replicated, may hold values from -6 to 6
- prop_phase: float32 [256, 256], replicated, may hold values from -3.140625 to 3.140625
- row_off: int32 [64], P('tile'), may hold values from 0 to 255
- col_off: int32 [64], P('tile'), may hold values from 0 to 768
- measured: float32 [64, 256, 256], P('tile'), may hold values from 0 to 1.6
Outputs:
- obj_grad: float32 [4, 2, 16384, 1024], P('cuts', None, 'tile')
The draws below stay inside these ranges and needn't reach their ends.
All inputs are finite; a program needn't handle non-finite values.
Results may differ from the reference program's by a relative error of at most 0.0003.
Values sent between devices are 32-bit elements; how exact they have to be, the bound alone decides.
A program may use at most 64 MiB of HBM per device.

```python
import jax
import jax.numpy as jnp
from jax import lax

WIN = 256
OBJ_COLS = 1024
STRIP_ROWS = 256
POS_DEV = 1
SLICES = 4
OBJ_ROWS = 16384
POSITIONS = 64


def draw_transmission(key, part):
    shape = (SLICES, 2, OBJ_ROWS, OBJ_COLS)
    noise = 0.2 * jax.random.normal(key, shape, jnp.float32)
    offset = jnp.array([0.95, 0.0], jnp.float32).reshape(1, 2, 1, 1)
    return offset + noise


def set_ends(drawn, key, smallest, largest):
    place = [jax.random.randint(jax.random.fold_in(key, axis), (), 0, length) for axis, length in enumerate(drawn.shape)]
    main_axis = drawn.shape.index(max(drawn.shape))
    neighbour = place[:main_axis] + [(place[main_axis] + 1) % drawn.shape[main_axis]] + place[main_axis + 1:]
    return drawn.at[tuple(place)].set(smallest).at[tuple(neighbour)].set(largest)


def levels(rng, shape, cuts, low, largest):
    factor_of, own = 1.0, jax.random.fold_in(rng, 6)
    for axis_at, blocks in cuts:
        heights = jnp.exp(jax.random.uniform(jax.random.fold_in(own, axis_at), (blocks,), jnp.float32, low / len(cuts), largest / len(cuts)))
        factor_of = factor_of * jnp.repeat(heights, shape[axis_at] // blocks).reshape([-1 if axis == axis_at else 1 for axis in range(len(shape))])
    return factor_of


def centred(rng, extent, scale, limit, kind=jnp.bfloat16):
    return jnp.clip(scale * jax.random.normal(rng, extent, jnp.float32), -limit, limit).astype(kind)


def setup_inputs(seed: int = 0) -> dict:
    key_of = jax.random.split(jax.random.key(seed), 7)
    transmission = draw_transmission(jax.random.fold_in(key_of[6], 71), 0)
    probe = centred(key_of[1], (2, WIN, WIN), 0.7071, 6.0, jnp.float32)
    prop_phase = jnp.clip(jax.random.uniform(key_of[2], (WIN, WIN), jnp.float32, -3.140625, 3.140625), -3.140625, 3.140625)
    row_off = set_ends(jax.random.randint(key_of[3], (POSITIONS,), 0, STRIP_ROWS), jax.random.fold_in(key_of[3], 1), 0, STRIP_ROWS - 1).astype(jnp.int32)
    col_off = set_ends(jax.random.randint(key_of[4], (POSITIONS,), 0, OBJ_COLS - WIN + 1), jax.random.fold_in(key_of[4], 1), 0, OBJ_COLS - WIN).astype(jnp.int32)
    measured = jnp.clip(1.6 * jax.random.uniform(key_of[5], (POSITIONS, WIN, WIN), jnp.float32) ** levels(key_of[5], (POSITIONS, WIN, WIN), ((0, 64),), -0.2, 0.2), 0.0, 1.6)
    return {"transmission": transmission, "probe": probe, "prop_phase": prop_phase, "row_off": row_off, "col_off": col_off, "measured": measured}


def forward_fft(field):
    return jnp.fft.fft2(field, norm="ortho")


def inverse_fft(field):
    return jnp.fft.ifft2(field, norm="ortho")


def reference(transmission, probe, prop_phase, row_off, col_off, measured):
    total_rows = transmission.shape[2]
    padded = jnp.pad(transmission, ((0, 0), (0, 0), (0, WIN), (0, 0)))
    kernel = jnp.exp(1j * prop_phase)
    probe_wave = probe[0] + 1j * probe[1]
    strips = jnp.arange(POSITIONS, dtype=jnp.int32) // POS_DEV
    top_rows = (strips * STRIP_ROWS + row_off).astype(jnp.int32)
    zero = jnp.zeros((), jnp.int32)

    def accumulate(gradient, inputs):
        row, column, intensity = inputs
        start = (zero, zero, row, column)
        patch = lax.dynamic_slice(padded, start, (SLICES, 2, WIN, WIN))
        layers_complex = patch[:, 0] + 1j * patch[:, 1]
        wave = probe_wave
        saved = []
        for layer in range(SLICES):
            saved.append(wave)
            wave = inverse_fft(kernel * forward_fft(wave * layers_complex[layer]))
        far = forward_fft(wave)
        residual = jnp.real(far) ** 2 + jnp.imag(far) ** 2 - intensity
        back = inverse_fft(residual * far)
        pieces = [None] * SLICES
        for layer in range(SLICES - 1, -1, -1):
            inner = inverse_fft(jnp.conj(kernel) * forward_fft(back))
            pieces[layer] = jnp.conj(saved[layer]) * inner
            back = jnp.conj(layers_complex[layer]) * inner
        stacked = jnp.stack(pieces, axis=0)
        piece = jnp.stack([jnp.real(stacked), jnp.imag(stacked)], axis=1)
        current = lax.dynamic_slice(gradient, start, piece.shape)
        gradient = lax.dynamic_update_slice(gradient, current + piece.astype(gradient.dtype), start)
        return gradient, None

    initial = jnp.zeros(padded.shape, jnp.float32)
    gradient, _ = lax.scan(accumulate, initial, (top_rows, col_off, measured))
    return gradient[:, :, :total_rows]
```

```python
import jax
import jax.numpy as jnp
from jax import lax
from jax.sharding import PartitionSpec as P

precise = lax.Precision.HIGHEST


def shifted(value, axis, by):
    devices = lax.axis_size(axis)
    pairs = [(i, i + by) for i in range(devices) if 0 <= i + by < devices]
    return lax.ppermute(value, axis, pairs)


def rotated(value, axis, by):
    devices = lax.axis_size(axis)
    pairs = [(i, (i + by) % devices) for i in range(devices)]
    return lax.ppermute(value, axis, pairs)


def dft_tables(length):
    index = lax.iota(jnp.int32, length)
    product = index[:, None] * index[None, :] % length
    angle = product.astype(jnp.float32) * (2.0 * jnp.pi / length)
    factor = 1.0 / jnp.sqrt(jnp.float32(length))
    return (jnp.cos(angle) * factor, jnp.sin(angle) * factor)


def stacked_tables(cosines, sines, direction):
    signed = sines * direction
    left = jnp.concatenate(
        [jnp.concatenate([cosines, -signed], axis=1), jnp.concatenate([signed, cosines], axis=1)],
        axis=0,
    )
    right = jnp.concatenate([cosines, signed], axis=1)
    return left, right


def transform(stacked, tables):
    left, right = tables
    width = right.shape[0]
    middle = jnp.dot(left, stacked, precision=precise)
    products = jnp.dot(middle, right, precision=precise)
    out_real = products[:width, :width] - products[width:, width:]
    out_imag = products[:width, width:] + products[width:, :width]
    return out_real, out_imag


def stack(real_part, imag_part):
    return jnp.concatenate([real_part, imag_part], axis=0)


def propagate(real_part, imag_part, forward, inverse, kernel_real, kernel_imag):
    freq_real, freq_imag = transform(stack(real_part, imag_part), forward)
    prod_real = freq_real * kernel_real - freq_imag * kernel_imag
    prod_imag = freq_real * kernel_imag + freq_imag * kernel_real
    return transform(stack(prod_real, prod_imag), inverse)


def per_device(transmission, probe, prop_phase, row_off, col_off, measured):
    rows = transmission.shape[2]
    columns = transmission.shape[3]
    width = probe.shape[1]
    sections = lax.axis_size("cuts")
    cut_index = lax.axis_index("cuts")
    cosines, sines = dft_tables(width)
    forward = stacked_tables(cosines, sines, -1.0)
    inverse = stacked_tables(cosines, sines, 1.0)
    kernel_real = jnp.cos(prop_phase)
    kernel_imag = jnp.sin(prop_phase)
    zero = jnp.zeros((), jnp.int32)
    row = row_off[0]
    column = col_off[0]
    column_above = shifted(col_off, "tile", 1)[0]

    band = shifted(transmission, "tile", -1)
    whole = jnp.concatenate([transmission, band], axis=2)
    patch = lax.dynamic_slice(whole, (zero, zero, row, column), (1, 2, width, width))[0]

    have = [patch] + [rotated(patch, "cuts", k) for k in range(1, sections)]
    have = jnp.stack(have, axis=0)
    order = (cut_index - lax.iota(jnp.int32, sections)) % sections
    layers = jnp.take(have, order, axis=0)

    wave_real = probe[0]
    wave_imag = probe[1]
    saved = []
    for layer in range(sections):
        saved.append((wave_real, wave_imag))
        layer_real = layers[layer, 0]
        layer_imag = layers[layer, 1]
        mixed_real = wave_real * layer_real - wave_imag * layer_imag
        mixed_imag = wave_real * layer_imag + wave_imag * layer_real
        wave_real, wave_imag = propagate(
            mixed_real, mixed_imag, forward, inverse, kernel_real, kernel_imag
        )
    far_real, far_imag = transform(stack(wave_real, wave_imag), forward)
    residual = far_real * far_real + far_imag * far_imag - measured[0]
    grad_real, grad_imag = transform(stack(residual * far_real, residual * far_imag), inverse)
    pieces = [None] * sections
    for layer in range(sections - 1, -1, -1):
        inner_real, inner_imag = propagate(
            grad_real, grad_imag, forward, inverse, kernel_real, -kernel_imag
        )
        wave_real, wave_imag = saved[layer]
        pieces[layer] = jnp.stack(
            [wave_real * inner_real + wave_imag * inner_imag,
             wave_real * inner_imag - wave_imag * inner_real],
            axis=0,
        )
        if layer > 0:
            layer_real = layers[layer, 0]
            layer_imag = layers[layer, 1]
            grad_real = layer_real * inner_real + layer_imag * inner_imag
            grad_imag = layer_real * inner_imag - layer_imag * inner_real
    piece = jnp.take(jnp.stack(pieces, axis=0), cut_index, axis=0)

    padded = jnp.concatenate([piece, jnp.zeros_like(piece)], axis=1)
    spill = lax.dynamic_slice(padded, (zero, rows - row, zero), (2, width, width))
    arrived = shifted(spill, "tile", 1)

    buffer = jnp.zeros((2, rows + width, columns), jnp.float32)
    buffer = lax.dynamic_update_slice(buffer, piece, (zero, row, column))
    result = buffer[:, :rows, :]
    current = lax.dynamic_slice(result, (zero, zero, column_above), (2, width, width))
    result = lax.dynamic_update_slice(result, current + arrived, (zero, zero, column_above))
    return result[None]


def solution(mesh):
    placed = (P("cuts", None, "tile", None), P(), P(), P("tile"), P("tile"), P("tile", None, None))
    return jax.shard_map(
        per_device,
        mesh=mesh,
        in_specs=placed,
        out_specs=P("cuts", None, "tile", None),
        check_vma=False,
    )
```

```python
import jax
import jax.numpy as jnp
from jax import lax
from jax.sharding import PartitionSpec as P


def shifted(value, axis, by):
    devices = lax.axis_size(axis)
    pairs = [(i, i + by) for i in range(devices) if 0 <= i + by < devices]
    return lax.ppermute(value, axis, pairs)


def rotated(value, axis, by):
    devices = lax.axis_size(axis)
    pairs = [(i, (i + by) % devices) for i in range(devices)]
    return lax.ppermute(value, axis, pairs)


def dft_tables(length):
    index = lax.iota(jnp.int32, length)
    product = index[:, None] * index[None, :] % length
    angle = product.astype(jnp.float32) * (2.0 * jnp.pi / length)
    factor = 1.0 / jnp.sqrt(jnp.float32(length))
    return (jnp.cos(angle) * factor, jnp.sin(angle) * factor)


def halves(value):
    scaled = value * jnp.float32(65537.0)
    high = scaled - (scaled - value)
    low = value - high
    return high.astype(jnp.bfloat16), low.astype(jnp.bfloat16)


def stacked_tables(cosines, sines, direction):
    signed = sines * direction
    left = jnp.concatenate(
        [jnp.concatenate([cosines, -signed], axis=1), jnp.concatenate([signed, cosines], axis=1)],
        axis=0,
    )
    right = jnp.concatenate([cosines, signed], axis=1)
    left_high, left_low = halves(left)
    right_high, right_low = halves(right)
    left_split = jnp.concatenate([left_high, left_high, left_low], axis=1)
    right_split = jnp.concatenate([right_high, right_low, right_high], axis=0)
    return left_split, right_split


def split_dot(split_table, value, table_first):
    high, low = halves(value)
    if table_first:
        operand = jnp.concatenate([high, low, high], axis=0)
        return jnp.dot(split_table, operand, preferred_element_type=jnp.float32)
    operand = jnp.concatenate([high, high, low], axis=1)
    return jnp.dot(operand, split_table, preferred_element_type=jnp.float32)


def transform(stacked, tables):
    left, right = tables
    width = right.shape[1] // 2
    middle = split_dot(left, stacked, True)
    products = split_dot(right, middle, False)
    out_real = products[:width, :width] - products[width:, width:]
    out_imag = products[:width, width:] + products[width:, :width]
    return out_real, out_imag


def stack(real_part, imag_part):
    return jnp.concatenate([real_part, imag_part], axis=0)


def propagate(real_part, imag_part, forward, inverse, kernel_real, kernel_imag):
    freq_real, freq_imag = transform(stack(real_part, imag_part), forward)
    prod_real = freq_real * kernel_real - freq_imag * kernel_imag
    prod_imag = freq_real * kernel_imag + freq_imag * kernel_real
    return transform(stack(prod_real, prod_imag), inverse)


def per_device(transmission, probe, prop_phase, row_off, col_off, measured):
    rows = transmission.shape[2]
    columns = transmission.shape[3]
    width = probe.shape[1]
    sections = lax.axis_size("cuts")
    cut_index = lax.axis_index("cuts")
    cosines, sines = dft_tables(width)
    forward = stacked_tables(cosines, sines, -1.0)
    inverse = stacked_tables(cosines, sines, 1.0)
    kernel_real = jnp.cos(prop_phase)
    kernel_imag = jnp.sin(prop_phase)
    zero = jnp.zeros((), jnp.int32)
    row = row_off[0]
    column = col_off[0]
    column_above = shifted(col_off, "tile", 1)[0]

    band = shifted(transmission, "tile", -1)
    whole = jnp.concatenate([transmission, band], axis=2)
    patch = lax.dynamic_slice(whole, (zero, zero, row, column), (1, 2, width, width))[0]

    have = [patch] + [rotated(patch, "cuts", k) for k in range(1, sections)]
    have = jnp.stack(have, axis=0)
    order = (cut_index - lax.iota(jnp.int32, sections)) % sections
    layers = jnp.take(have, order, axis=0)

    wave_real = probe[0]
    wave_imag = probe[1]
    saved = []
    for layer in range(sections):
        saved.append((wave_real, wave_imag))
        layer_real = layers[layer, 0]
        layer_imag = layers[layer, 1]
        mixed_real = wave_real * layer_real - wave_imag * layer_imag
        mixed_imag = wave_real * layer_imag + wave_imag * layer_real
        wave_real, wave_imag = propagate(
            mixed_real, mixed_imag, forward, inverse, kernel_real, kernel_imag
        )
    far_real, far_imag = transform(stack(wave_real, wave_imag), forward)
    residual = far_real * far_real + far_imag * far_imag - measured[0]
    grad_real, grad_imag = transform(stack(residual * far_real, residual * far_imag), inverse)
    pieces = [None] * sections
    for layer in range(sections - 1, -1, -1):
        inner_real, inner_imag = propagate(
            grad_real, grad_imag, forward, inverse, kernel_real, -kernel_imag
        )
        wave_real, wave_imag = saved[layer]
        pieces[layer] = jnp.stack(
            [wave_real * inner_real + wave_imag * inner_imag,
             wave_real * inner_imag - wave_imag * inner_real],
            axis=0,
        )
        if layer > 0:
            layer_real = layers[layer, 0]
            layer_imag = layers[layer, 1]
            grad_real = layer_real * inner_real + layer_imag * inner_imag
            grad_imag = layer_real * inner_imag - layer_imag * inner_real
    piece = jnp.take(jnp.stack(pieces, axis=0), cut_index, axis=0)

    padded = jnp.concatenate([piece, jnp.zeros_like(piece)], axis=1)
    spill = lax.dynamic_slice(padded, (zero, rows - row, zero), (2, width, width))
    arrived = shifted(spill, "tile", 1)

    own = jnp.pad(piece, ((0, 0), (rows, rows), (columns, columns)))
    own = lax.dynamic_slice(own, (zero, rows - row, columns - column), (2, rows, columns))
    above = jnp.pad(arrived, ((0, 0), (0, rows), (columns, columns)))
    above = lax.dynamic_slice(above, (zero, zero, columns - column_above), (2, rows, columns))
    result = own + above
    return result[None]


def solution(mesh):
    placed = (P("cuts", None, "tile", None), P(), P(), P("tile"), P("tile"), P("tile", None, None))
    return jax.shard_map(
        per_device,
        mesh=mesh,
        in_specs=placed,
        out_specs=P("cuts", None, "tile", None),
        check_vma=False,
    )
```

```python
import jax
import jax.numpy as jnp
from jax import lax
from jax.sharding import PartitionSpec as P


def shifted(value, axis, by):
    devices = lax.axis_size(axis)
    pairs = [(i, i + by) for i in range(devices) if 0 <= i + by < devices]
    return lax.ppermute(value, axis, pairs)


def rotated(value, axis, by):
    devices = lax.axis_size(axis)
    pairs = [(i, (i + by) % devices) for i in range(devices)]
    return lax.ppermute(value, axis, pairs)


def dft_tables(length):
    index = lax.iota(jnp.int32, length)
    product = index[:, None] * index[None, :] % length
    angle = product.astype(jnp.float32) * (2.0 * jnp.pi / length)
    factor = 1.0 / jnp.sqrt(jnp.float32(length))
    return (jnp.cos(angle) * factor, jnp.sin(angle) * factor)


def halves(value):
    scaled = value * jnp.float32(65537.0)
    high = scaled - (scaled - value)
    low = value - high
    return high.astype(jnp.bfloat16), low.astype(jnp.bfloat16)


def stacked_tables(cosines, sines, direction):
    signed = sines * direction
    left = jnp.concatenate(
        [jnp.concatenate([cosines, -signed], axis=1), jnp.concatenate([signed, cosines], axis=1)],
        axis=0,
    )
    right = jnp.concatenate([cosines, signed], axis=1)
    left_high, left_low = halves(left)
    right_high, right_low = halves(right)
    left_split = jnp.concatenate([left_high, left_high, left_low], axis=1)
    right_split = jnp.concatenate([right_high, right_low, right_high], axis=0)
    return left_split, right_split


def split_dot(split_table, value, table_first):
    high, low = halves(value)
    if table_first:
        operand = jnp.concatenate([high, low, high], axis=0)
        return jnp.dot(split_table, operand, preferred_element_type=jnp.float32)
    operand = jnp.concatenate([high, high, low], axis=1)
    return jnp.dot(operand, split_table, preferred_element_type=jnp.float32)


def transform(stacked, tables):
    left, right = tables
    width = right.shape[1] // 2
    middle = split_dot(left, stacked, True)
    products = split_dot(right, middle, False)
    out_real = products[:width, :width] - products[width:, width:]
    out_imag = products[:width, width:] + products[width:, :width]
    return out_real, out_imag


def stack(real_part, imag_part):
    return jnp.concatenate([real_part, imag_part], axis=0)


def propagate(real_part, imag_part, forward, inverse, kernel_real, kernel_imag):
    freq_real, freq_imag = transform(stack(real_part, imag_part), forward)
    prod_real = freq_real * kernel_real - freq_imag * kernel_imag
    prod_imag = freq_real * kernel_imag + freq_imag * kernel_real
    return transform(stack(prod_real, prod_imag), inverse)


def per_device(transmission, probe, prop_phase, row_off, col_off, measured):
    rows = transmission.shape[2]
    columns = transmission.shape[3]
    width = probe.shape[1]
    sections = lax.axis_size("cuts")
    cut_index = lax.axis_index("cuts")
    cosines, sines = dft_tables(width)
    forward = stacked_tables(cosines, sines, -1.0)
    inverse = stacked_tables(cosines, sines, 1.0)
    kernel_real = jnp.cos(prop_phase)
    kernel_imag = jnp.sin(prop_phase)
    zero = jnp.zeros((), jnp.int32)
    row = row_off[0]
    column = col_off[0]
    offsets_above = shifted(jnp.stack([row, column]), "tile", 1)
    row_above = offsets_above[0]
    column_above = offsets_above[1]

    strip = transmission[0]
    lent = lax.dynamic_slice(strip, (zero, zero, column_above), (2, width, width))
    lent = jnp.pad(lent, ((0, 0), (width, 0), (0, 0)))
    lent = lax.dynamic_slice(lent, (zero, row_above, zero), (2, width, width))
    borrowed = shifted(lent, "tile", -1)
    kept = jnp.pad(strip, ((0, 0), (0, width), (0, 0)))
    kept = lax.dynamic_slice(kept, (zero, row, column), (2, width, width))
    window = kept + borrowed

    layers = []
    for layer in range(sections):
        total = jnp.where(cut_index == layer, window, jnp.zeros_like(window))
        for step in range(1, sections):
            total = total + lax.ppermute(window, "cuts", [(layer, (layer + step) % sections)])
        layers.append(total)

    wave_real = probe[0]
    wave_imag = probe[1]
    saved = []
    for layer in range(sections):
        saved.append((wave_real, wave_imag))
        layer_real = layers[layer][0]
        layer_imag = layers[layer][1]
        mixed_real = wave_real * layer_real - wave_imag * layer_imag
        mixed_imag = wave_real * layer_imag + wave_imag * layer_real
        wave_real, wave_imag = propagate(
            mixed_real, mixed_imag, forward, inverse, kernel_real, kernel_imag
        )
    far_real, far_imag = transform(stack(wave_real, wave_imag), forward)
    residual = far_real * far_real + far_imag * far_imag - measured[0]
    grad_real, grad_imag = transform(stack(residual * far_real, residual * far_imag), inverse)
    pieces = [None] * sections
    for layer in range(sections - 1, -1, -1):
        inner_real, inner_imag = propagate(
            grad_real, grad_imag, forward, inverse, kernel_real, -kernel_imag
        )
        wave_real, wave_imag = saved[layer]
        pieces[layer] = jnp.stack(
            [wave_real * inner_real + wave_imag * inner_imag,
             wave_real * inner_imag - wave_imag * inner_real],
            axis=0,
        )
        if layer > 0:
            layer_real = layers[layer][0]
            layer_imag = layers[layer][1]
            grad_real = layer_real * inner_real + layer_imag * inner_imag
            grad_imag = layer_real * inner_imag - layer_imag * inner_real
    piece = jnp.take(jnp.stack(pieces, axis=0), cut_index, axis=0)

    padded = jnp.concatenate([piece, jnp.zeros_like(piece)], axis=1)
    spill = lax.dynamic_slice(padded, (zero, rows - row, zero), (2, width, width))
    arrived = shifted(spill, "tile", 1)

    own = jnp.pad(piece, ((0, 0), (rows, rows), (columns, columns)))
    own = lax.dynamic_slice(own, (zero, rows - row, columns - column), (2, rows, columns))
    above = jnp.pad(arrived, ((0, 0), (0, rows), (columns, columns)))
    above = lax.dynamic_slice(above, (zero, zero, columns - column_above), (2, rows, columns))
    result = own + above
    return result[None]


def solution(mesh):
    placed = (P("cuts", None, "tile", None), P(), P(), P("tile"), P("tile"), P("tile", None, None))
    return jax.shard_map(
        per_device,
        mesh=mesh,
        in_specs=placed,
        out_specs=P("cuts", None, "tile", None),
        check_vma=False,
    )
```

```python
import jax
import jax.numpy as jnp
from jax import lax
from jax.sharding import PartitionSpec as P


def shifted(value, axis, by):
    devices = lax.axis_size(axis)
    pairs = [(i, i + by) for i in range(devices) if 0 <= i + by < devices]
    return lax.ppermute(value, axis, pairs)


def rotated(value, axis, by):
    devices = lax.axis_size(axis)
    pairs = [(i, (i + by) % devices) for i in range(devices)]
    return lax.ppermute(value, axis, pairs)


def dft_tables(length):
    index = lax.iota(jnp.int32, length)
    product = index[:, None] * index[None, :] % length
    angle = product.astype(jnp.float32) * (2.0 * jnp.pi / length)
    factor = 1.0 / jnp.sqrt(jnp.float32(length))
    return (jnp.cos(angle) * factor, jnp.sin(angle) * factor)


def halves(value):
    scaled = value * jnp.float32(65537.0)
    high = scaled - (scaled - value)
    low = value - high
    return high.astype(jnp.bfloat16), low.astype(jnp.bfloat16)


def stacked_tables(cosines, sines, direction):
    signed = sines * direction
    left = jnp.concatenate(
        [jnp.concatenate([cosines, -signed], axis=1), jnp.concatenate([signed, cosines], axis=1)],
        axis=0,
    )
    right = jnp.concatenate([cosines, signed], axis=1)
    left_high, left_low = halves(left)
    right_high, right_low = halves(right)
    left_split = jnp.concatenate([left_high, left_high, left_low], axis=1)
    right_split = jnp.concatenate([right_high, right_low, right_high], axis=0)
    return left_split, right_split


def split_dot(split_table, value, table_first):
    high, low = halves(value)
    if table_first:
        operand = jnp.concatenate([high, low, high], axis=0)
        return jnp.dot(split_table, operand, preferred_element_type=jnp.float32)
    operand = jnp.concatenate([high, high, low], axis=1)
    return jnp.dot(operand, split_table, preferred_element_type=jnp.float32)


def transform(stacked, tables):
    left, right = tables
    width = right.shape[1] // 2
    middle = split_dot(left, stacked, True)
    products = split_dot(right, middle, False)
    out_real = products[:width, :width] - products[width:, width:]
    out_imag = products[:width, width:] + products[width:, :width]
    return out_real, out_imag


def stack(real_part, imag_part):
    return jnp.concatenate([real_part, imag_part], axis=0)


def propagate(real_part, imag_part, forward, inverse, kernel_real, kernel_imag):
    freq_real, freq_imag = transform(stack(real_part, imag_part), forward)
    prod_real = freq_real * kernel_real - freq_imag * kernel_imag
    prod_imag = freq_real * kernel_imag + freq_imag * kernel_real
    return transform(stack(prod_real, prod_imag), inverse)


def per_device(transmission, probe, prop_phase, row_off, col_off, measured):
    rows = transmission.shape[2]
    columns = transmission.shape[3]
    width = probe.shape[1]
    sections = lax.axis_size("cuts")
    cut_index = lax.axis_index("cuts")
    cosines, sines = dft_tables(width)
    forward = stacked_tables(cosines, sines, -1.0)
    inverse = stacked_tables(cosines, sines, 1.0)
    kernel_real = jnp.cos(prop_phase)
    kernel_imag = jnp.sin(prop_phase)
    zero = jnp.zeros((), jnp.int32)
    row = row_off[0]
    column = col_off[0]
    offsets_above = shifted(jnp.stack([row, column]), "tile", 1)
    row_above = offsets_above[0]
    column_above = offsets_above[1]

    strip = transmission[0]
    lent = lax.dynamic_slice(strip, (zero, zero, column_above), (2, width, width))
    lent = jnp.pad(lent, ((0, 0), (width, 0), (0, 0)))
    lent = lax.dynamic_slice(lent, (zero, row_above, zero), (2, width, width))
    borrowed = shifted(lent, "tile", -1)
    kept = jnp.pad(strip, ((0, 0), (0, width), (0, 0)))
    kept = lax.dynamic_slice(kept, (zero, row, column), (2, width, width))
    window = kept + borrowed

    have = [window] + [rotated(window, "cuts", k) for k in range(1, sections)]
    have = jnp.stack(have, axis=0)
    order = (cut_index - lax.iota(jnp.int32, sections)) % sections
    layers = jnp.take(have, order, axis=0)

    wave_real = probe[0]
    wave_imag = probe[1]
    saved = []
    for layer in range(sections):
        saved.append((wave_real, wave_imag))
        layer_real = layers[layer][0]
        layer_imag = layers[layer][1]
        mixed_real = wave_real * layer_real - wave_imag * layer_imag
        mixed_imag = wave_real * layer_imag + wave_imag * layer_real
        wave_real, wave_imag = propagate(
            mixed_real, mixed_imag, forward, inverse, kernel_real, kernel_imag
        )
    far_real, far_imag = transform(stack(wave_real, wave_imag), forward)
    residual = far_real * far_real + far_imag * far_imag - measured[0]
    grad_real, grad_imag = transform(stack(residual * far_real, residual * far_imag), inverse)
    pieces = [None] * sections
    for layer in range(sections - 1, -1, -1):
        inner_real, inner_imag = propagate(
            grad_real, grad_imag, forward, inverse, kernel_real, -kernel_imag
        )
        wave_real, wave_imag = saved[layer]
        pieces[layer] = jnp.stack(
            [wave_real * inner_real + wave_imag * inner_imag,
             wave_real * inner_imag - wave_imag * inner_real],
            axis=0,
        )
        if layer > 0:
            layer_real = layers[layer][0]
            layer_imag = layers[layer][1]
            grad_real = layer_real * inner_real + layer_imag * inner_imag
            grad_imag = layer_real * inner_imag - layer_imag * inner_real
    piece = jnp.take(jnp.stack(pieces, axis=0), cut_index, axis=0)

    padded = jnp.concatenate([piece, jnp.zeros_like(piece)], axis=1)
    spill = lax.dynamic_slice(padded, (zero, rows - row, zero), (2, width, width))
    arrived = shifted(spill, "tile", 1)

    own = jnp.pad(piece, ((0, 0), (rows, rows), (columns, columns)))
    own = lax.dynamic_slice(own, (zero, rows - row, columns - column), (2, rows, columns))
    above = jnp.pad(arrived, ((0, 0), (0, rows), (columns, columns)))
    above = lax.dynamic_slice(above, (zero, zero, columns - column_above), (2, rows, columns))
    result = own + above
    return result[None]


def solution(mesh):
    placed = (P("cuts", None, "tile", None), P(), P(), P("tile"), P("tile"), P("tile", None, None))
    return jax.shard_map(
        per_device,
        mesh=mesh,
        in_specs=placed,
        out_specs=P("cuts", None, "tile", None),
        check_vma=False,
    )
```

```python
import jax
import jax.numpy as jnp
from jax import lax
from jax.sharding import PartitionSpec as P


def shifted(value, axis, by):
    devices = lax.axis_size(axis)
    pairs = [(i, i + by) for i in range(devices) if 0 <= i + by < devices]
    return lax.ppermute(value, axis, pairs)


def rotated(value, axis, by):
    devices = lax.axis_size(axis)
    pairs = [(i, (i + by) % devices) for i in range(devices)]
    return lax.ppermute(value, axis, pairs)


def dft_tables(length):
    index = lax.iota(jnp.int32, length)
    product = index[:, None] * index[None, :] % length
    angle = product.astype(jnp.float32) * (2.0 * jnp.pi / length)
    factor = 1.0 / jnp.sqrt(jnp.float32(length))
    return (jnp.cos(angle) * factor, jnp.sin(angle) * factor)


def halves(value):
    scaled = value * jnp.float32(65537.0)
    high = scaled - (scaled - value)
    low = value - high
    return high.astype(jnp.bfloat16), low.astype(jnp.bfloat16)


def stacked_tables(cosines, sines, direction):
    signed = sines * direction
    left = jnp.concatenate(
        [jnp.concatenate([cosines, -signed], axis=1), jnp.concatenate([signed, cosines], axis=1)],
        axis=0,
    )
    right = jnp.concatenate([cosines, signed], axis=1)
    left_high, left_low = halves(left)
    right_high, right_low = halves(right)
    left_split = jnp.concatenate([left_high, left_high, left_low], axis=1)
    right_split = jnp.concatenate([right_high, right_low, right_high], axis=0)
    return left_split, right_split


def split_dot(split_table, value, table_first):
    high, low = halves(value)
    if table_first:
        operand = jnp.concatenate([high, low, high], axis=0)
        return jnp.dot(split_table, operand, preferred_element_type=jnp.float32)
    operand = jnp.concatenate([high, high, low], axis=1)
    return jnp.dot(operand, split_table, preferred_element_type=jnp.float32)


def transform(stacked, tables):
    left, right = tables
    width = right.shape[1] // 2
    middle = split_dot(left, stacked, True)
    products = split_dot(right, middle, False)
    out_real = products[:width, :width] - products[width:, width:]
    out_imag = products[:width, width:] + products[width:, :width]
    return out_real, out_imag


def stack(real_part, imag_part):
    return jnp.concatenate([real_part, imag_part], axis=0)


def propagate(real_part, imag_part, forward, inverse, kernel_real, kernel_imag):
    freq_real, freq_imag = transform(stack(real_part, imag_part), forward)
    prod_real = freq_real * kernel_real - freq_imag * kernel_imag
    prod_imag = freq_real * kernel_imag + freq_imag * kernel_real
    return transform(stack(prod_real, prod_imag), inverse)


def per_device(transmission, probe, prop_phase, row_off, col_off, measured):
    rows = transmission.shape[2]
    columns = transmission.shape[3]
    width = probe.shape[1]
    sections = lax.axis_size("cuts")
    cut_index = lax.axis_index("cuts")
    cosines, sines = dft_tables(width)
    forward = stacked_tables(cosines, sines, -1.0)
    inverse = stacked_tables(cosines, sines, 1.0)
    kernel_real = jnp.cos(prop_phase)
    kernel_imag = jnp.sin(prop_phase)
    zero = jnp.zeros((), jnp.int32)
    row = row_off[0]
    column = col_off[0]
    offsets_above = shifted(jnp.stack([row, column]), "tile", 1)
    row_above = offsets_above[0]
    column_above = offsets_above[1]

    strip = transmission[0]
    lent = lax.dynamic_slice(strip, (zero, zero, column_above), (2, width, width))
    lent = jnp.pad(lent, ((0, 0), (width, 0), (0, 0)))
    lent = lax.dynamic_slice(lent, (zero, row_above, zero), (2, width, width))
    borrowed = shifted(lent, "tile", -1)
    kept = jnp.pad(strip, ((0, 0), (0, width), (0, 0)))
    kept = lax.dynamic_slice(kept, (zero, row, column), (2, width, width))
    window = kept + borrowed

    if sections == 4:
        from_left = rotated(window, "cuts", 1)
        from_right = rotated(window, "cuts", -1)
        far_real = rotated(from_right[0], "cuts", -1)
        far_imag = rotated(from_left[1], "cuts", 1)
        have = [window, from_left, jnp.stack([far_real, far_imag], axis=0), from_right]
    else:
        have = [window] + [rotated(window, "cuts", k) for k in range(1, sections)]
    layers = [
        lax.select_n((cut_index - layer) % sections, *have) for layer in range(sections)
    ]

    wave_real = probe[0]
    wave_imag = probe[1]
    saved = []
    for layer in range(sections):
        saved.append((wave_real, wave_imag))
        layer_real = layers[layer][0]
        layer_imag = layers[layer][1]
        mixed_real = wave_real * layer_real - wave_imag * layer_imag
        mixed_imag = wave_real * layer_imag + wave_imag * layer_real
        wave_real, wave_imag = propagate(
            mixed_real, mixed_imag, forward, inverse, kernel_real, kernel_imag
        )
    far_real, far_imag = transform(stack(wave_real, wave_imag), forward)
    residual = far_real * far_real + far_imag * far_imag - measured[0]
    grad_real, grad_imag = transform(stack(residual * far_real, residual * far_imag), inverse)
    pieces = [None] * sections
    for layer in range(sections - 1, -1, -1):
        inner_real, inner_imag = propagate(
            grad_real, grad_imag, forward, inverse, kernel_real, -kernel_imag
        )
        wave_real, wave_imag = saved[layer]
        pieces[layer] = jnp.stack(
            [wave_real * inner_real + wave_imag * inner_imag,
             wave_real * inner_imag - wave_imag * inner_real],
            axis=0,
        )
        if layer > 0:
            layer_real = layers[layer][0]
            layer_imag = layers[layer][1]
            grad_real = layer_real * inner_real + layer_imag * inner_imag
            grad_imag = layer_real * inner_imag - layer_imag * inner_real
    piece = jnp.take(jnp.stack(pieces, axis=0), cut_index, axis=0)

    padded = jnp.concatenate([piece, jnp.zeros_like(piece)], axis=1)
    spill = lax.dynamic_slice(padded, (zero, rows - row, zero), (2, width, width))
    arrived = shifted(spill, "tile", 1)

    own = jnp.pad(piece, ((0, 0), (rows, rows), (columns, columns)))
    own = lax.dynamic_slice(own, (zero, rows - row, columns - column), (2, rows, columns))
    above = jnp.pad(arrived, ((0, 0), (0, rows), (columns, columns)))
    above = lax.dynamic_slice(above, (zero, zero, columns - column_above), (2, rows, columns))
    result = own + above
    return result[None]


def solution(mesh):
    placed = (P("cuts", None, "tile", None), P(), P(), P("tile"), P("tile"), P("tile", None, None))
    return jax.shard_map(
        per_device,
        mesh=mesh,
        in_specs=placed,
        out_specs=P("cuts", None, "tile", None),
        check_vma=False,
    )
```

```python
import jax
import jax.numpy as jnp
from jax import lax
from jax.sharding import PartitionSpec as P


def shifted(value, axis, by):
    devices = lax.axis_size(axis)
    pairs = [(i, i + by) for i in range(devices) if 0 <= i + by < devices]
    return lax.ppermute(value, axis, pairs)


def rotated(value, axis, by):
    devices = lax.axis_size(axis)
    pairs = [(i, (i + by) % devices) for i in range(devices)]
    return lax.ppermute(value, axis, pairs)


def dft_tables(length):
    index = lax.iota(jnp.int32, length)
    product = index[:, None] * index[None, :] % length
    angle = product.astype(jnp.float32) * (2.0 * jnp.pi / length)
    factor = 1.0 / jnp.sqrt(jnp.float32(length))
    return (jnp.cos(angle) * factor, jnp.sin(angle) * factor)


def halves(value):
    scaled = value * jnp.float32(65537.0)
    high = scaled - (scaled - value)
    low = value - high
    return high.astype(jnp.bfloat16), low.astype(jnp.bfloat16)


def stacked_tables(cosines, sines, direction):
    signed = sines * direction
    left = jnp.concatenate(
        [jnp.concatenate([cosines, -signed], axis=1), jnp.concatenate([signed, cosines], axis=1)],
        axis=0,
    )
    right = jnp.concatenate([cosines, signed], axis=1)
    left_high, left_low = halves(left)
    right_high, right_low = halves(right)
    left_split = jnp.concatenate([left_high, left_high, left_low], axis=1)
    right_split = jnp.concatenate([right_high, right_low, right_high], axis=0)
    return left_split, right_split


def split_dot(split_table, value, table_first):
    high, low = halves(value)
    if table_first:
        operand = jnp.concatenate([high, low, high], axis=0)
        return jnp.dot(split_table, operand, preferred_element_type=jnp.float32)
    operand = jnp.concatenate([high, high, low], axis=1)
    return jnp.dot(operand, split_table, preferred_element_type=jnp.float32)


def transform(stacked, tables):
    left, right = tables
    width = right.shape[1] // 2
    middle = split_dot(left, stacked, True)
    products = split_dot(right, middle, False)
    out_real = products[:width, :width] - products[width:, width:]
    out_imag = products[:width, width:] + products[width:, :width]
    return out_real, out_imag


def stack(real_part, imag_part):
    return jnp.concatenate([real_part, imag_part], axis=0)


def per_device(transmission, probe, prop_phase, row_off, col_off, measured):
    rows = transmission.shape[2]
    columns = transmission.shape[3]
    width = probe.shape[1]
    sections = lax.axis_size("cuts")
    cut_index = lax.axis_index("cuts")
    cosines, sines = dft_tables(width)
    forward = stacked_tables(cosines, sines, -1.0)
    inverse = stacked_tables(cosines, sines, 1.0)
    kernel_real = jnp.cos(prop_phase)
    kernel_imag = jnp.sin(prop_phase)
    zero = jnp.zeros((), jnp.int32)
    row = row_off[0]
    column = col_off[0]
    offsets_above = shifted(jnp.stack([row, column]), "tile", 1)
    row_above = offsets_above[0]
    column_above = offsets_above[1]

    strip = transmission[0]
    lent = lax.dynamic_slice(strip, (zero, zero, column_above), (2, width, width))
    lent = jnp.pad(lent, ((0, 0), (width, 0), (0, 0)))
    lent = lax.dynamic_slice(lent, (zero, row_above, zero), (2, width, width))
    borrowed = shifted(lent, "tile", -1)
    kept = jnp.pad(strip, ((0, 0), (0, width), (0, 0)))
    kept = lax.dynamic_slice(kept, (zero, row, column), (2, width, width))
    window = kept + borrowed

    if sections == 4:
        from_left = rotated(window, "cuts", 1)
        from_right = rotated(window, "cuts", -1)
        far_real = rotated(from_right[0], "cuts", -1)
        far_imag = rotated(from_left[1], "cuts", 1)
        have = [window, from_left, jnp.stack([far_real, far_imag], axis=0), from_right]
    else:
        have = [window] + [rotated(window, "cuts", k) for k in range(1, sections)]
    layers = [
        lax.select_n((cut_index - layer) % sections, *have) for layer in range(sections)
    ]

    wave_real = probe[0]
    wave_imag = probe[1]
    saved = []
    for layer in range(sections):
        saved.append((wave_real, wave_imag))
        layer_real = layers[layer][0]
        layer_imag = layers[layer][1]
        mixed_real = wave_real * layer_real - wave_imag * layer_imag
        mixed_imag = wave_real * layer_imag + wave_imag * layer_real
        freq_real, freq_imag = transform(stack(mixed_real, mixed_imag), forward)
        prod_real = freq_real * kernel_real - freq_imag * kernel_imag
        prod_imag = freq_real * kernel_imag + freq_imag * kernel_real
        if layer < sections - 1:
            wave_real, wave_imag = transform(stack(prod_real, prod_imag), inverse)
    far_real, far_imag = prod_real, prod_imag
    residual = far_real * far_real + far_imag * far_imag - measured[0]
    back_real = residual * far_real
    back_imag = residual * far_imag
    pieces = [None] * sections
    for layer in range(sections - 1, -1, -1):
        if layer < sections - 1:
            back_real, back_imag = transform(stack(grad_real, grad_imag), forward)
        prod_real = back_real * kernel_real + back_imag * kernel_imag
        prod_imag = back_imag * kernel_real - back_real * kernel_imag
        inner_real, inner_imag = transform(stack(prod_real, prod_imag), inverse)
        wave_real, wave_imag = saved[layer]
        pieces[layer] = jnp.stack(
            [wave_real * inner_real + wave_imag * inner_imag,
             wave_real * inner_imag - wave_imag * inner_real],
            axis=0,
        )
        if layer > 0:
            layer_real = layers[layer][0]
            layer_imag = layers[layer][1]
            grad_real = layer_real * inner_real + layer_imag * inner_imag
            grad_imag = layer_real * inner_imag - layer_imag * inner_real
    piece = jnp.take(jnp.stack(pieces, axis=0), cut_index, axis=0)

    padded = jnp.concatenate([piece, jnp.zeros_like(piece)], axis=1)
    spill = lax.dynamic_slice(padded, (zero, rows - row, zero), (2, width, width))
    arrived = shifted(spill, "tile", 1)

    own = jnp.pad(piece, ((0, 0), (rows, rows), (columns, columns)))
    own = lax.dynamic_slice(own, (zero, rows - row, columns - column), (2, rows, columns))
    above = jnp.pad(arrived, ((0, 0), (0, rows), (columns, columns)))
    above = lax.dynamic_slice(above, (zero, zero, columns - column_above), (2, rows, columns))
    result = own + above
    return result[None]


def solution(mesh):
    placed = (P("cuts", None, "tile", None), P(), P(), P("tile"), P("tile"), P("tile", None, None))
    return jax.shard_map(
        per_device,
        mesh=mesh,
        in_specs=placed,
        out_specs=P("cuts", None, "tile", None),
        check_vma=False,
    )
```

```python
import jax
import jax.numpy as jnp
from jax import lax
from jax.experimental import pallas as pl
from jax.experimental.pallas import tpu as pltpu
from jax.sharding import PartitionSpec as P


def shifted(value, axis, by):
    devices = lax.axis_size(axis)
    pairs = [(i, i + by) for i in range(devices) if 0 <= i + by < devices]
    return lax.ppermute(value, axis, pairs)


def rotated(value, axis, by):
    devices = lax.axis_size(axis)
    pairs = [(i, (i + by) % devices) for i in range(devices)]
    return lax.ppermute(value, axis, pairs)


def dft_tables(length):
    index = lax.iota(jnp.int32, length)
    product = index[:, None] * index[None, :] % length
    angle = product.astype(jnp.float32) * (2.0 * jnp.pi / length)
    factor = 1.0 / jnp.sqrt(jnp.float32(length))
    return (jnp.cos(angle) * factor, jnp.sin(angle) * factor)


def halves(value):
    scaled = value * jnp.float32(65537.0)
    high = scaled - (scaled - value)
    low = value - high
    return high.astype(jnp.bfloat16), low.astype(jnp.bfloat16)


def stacked_tables(cosines, sines, direction):
    signed = sines * direction
    left = jnp.concatenate(
        [jnp.concatenate([cosines, -signed], axis=1), jnp.concatenate([signed, cosines], axis=1)],
        axis=0,
    )
    right = jnp.concatenate([cosines, signed], axis=1)
    left_high, left_low = halves(left)
    right_high, right_low = halves(right)
    left_split = jnp.concatenate([left_high, left_high, left_low], axis=1)
    right_split = jnp.concatenate([right_high, right_low, right_high], axis=0)
    return left_split, right_split


def split_dot(split_table, value, table_first):
    high, low = halves(value)
    if table_first:
        operand = jnp.concatenate([high, low, high], axis=0)
        return jnp.dot(split_table, operand, preferred_element_type=jnp.float32)
    operand = jnp.concatenate([high, high, low], axis=1)
    return jnp.dot(operand, split_table, preferred_element_type=jnp.float32)


def transform(stacked, tables):
    left, right = tables
    width = right.shape[1] // 2
    middle = split_dot(left, stacked, True)
    products = split_dot(right, middle, False)
    out_real = products[:width, :width] - products[width:, width:]
    out_imag = products[:width, width:] + products[width:, :width]
    return out_real, out_imag


def stack(real_part, imag_part):
    return jnp.concatenate([real_part, imag_part], axis=0)


def exchange_kernel(window_ref, left_ref, right_ref, far_ref, send_sem, recv_sem):
    devices = lax.axis_size("cuts")
    me = lax.axis_index("cuts")
    right = lax.rem(me + 1, devices)
    left = lax.rem(me + devices - 1, devices)
    mesh_ids = pl.DeviceIdType.MESH
    barrier = pltpu.get_barrier_semaphore()
    for neighbour in (left, right):
        pl.semaphore_signal(barrier, inc=1, device_id={"cuts": neighbour}, device_id_type=mesh_ids)
    pl.semaphore_wait(barrier, 2)

    def remote(source, target, slot, neighbour):
        return pltpu.make_async_remote_copy(
            src_ref=source,
            dst_ref=target,
            send_sem=send_sem.at[slot],
            recv_sem=recv_sem.at[slot],
            device_id={"cuts": neighbour},
            device_id_type=mesh_ids,
        )

    to_right = remote(window_ref, left_ref, 0, right)
    to_left = remote(window_ref, right_ref, 1, left)
    to_right.start()
    to_left.start()
    to_right.wait()
    to_left.wait()
    far_real = remote(right_ref.at[0], far_ref.at[0], 2, left)
    far_imag = remote(left_ref.at[1], far_ref.at[1], 3, right)
    far_real.start()
    far_imag.start()
    far_real.wait()
    far_imag.wait()


def exchange(window):
    shape = jax.ShapeDtypeStruct(window.shape, window.dtype)
    vmem = pl.BlockSpec(memory_space=pltpu.VMEM)
    return pl.pallas_call(
        exchange_kernel,
        out_shape=(shape, shape, shape),
        in_specs=[vmem],
        out_specs=(vmem, vmem, vmem),
        scratch_shapes=[pltpu.SemaphoreType.DMA((4,)), pltpu.SemaphoreType.DMA((4,))],
        compiler_params=pltpu.CompilerParams(collective_id=0, has_side_effects=True),
    )(window)


def per_device(transmission, probe, prop_phase, row_off, col_off, measured):
    rows = transmission.shape[2]
    columns = transmission.shape[3]
    width = probe.shape[1]
    sections = lax.axis_size("cuts")
    cut_index = lax.axis_index("cuts")
    cosines, sines = dft_tables(width)
    forward = stacked_tables(cosines, sines, -1.0)
    inverse = stacked_tables(cosines, sines, 1.0)
    kernel_real = jnp.cos(prop_phase)
    kernel_imag = jnp.sin(prop_phase)
    zero = jnp.zeros((), jnp.int32)
    row = row_off[0]
    column = col_off[0]
    offsets_above = shifted(jnp.stack([row, column]), "tile", 1)
    row_above = offsets_above[0]
    column_above = offsets_above[1]

    strip = transmission[0]
    lent = lax.dynamic_slice(strip, (zero, zero, column_above), (2, width, width))
    lent = jnp.pad(lent, ((0, 0), (width, 0), (0, 0)))
    lent = lax.dynamic_slice(lent, (zero, row_above, zero), (2, width, width))
    borrowed = shifted(lent, "tile", -1)
    kept = jnp.pad(strip, ((0, 0), (0, width), (0, 0)))
    kept = lax.dynamic_slice(kept, (zero, row, column), (2, width, width))
    window = kept + borrowed

    if sections == 4:
        from_left, from_right, far = exchange(window)
        have = [window, from_left, far, from_right]
    else:
        have = [window] + [rotated(window, "cuts", k) for k in range(1, sections)]
    layers = [
        lax.select_n((cut_index - layer) % sections, *have) for layer in range(sections)
    ]

    wave_real = probe[0]
    wave_imag = probe[1]
    saved = []
    for layer in range(sections):
        saved.append((wave_real, wave_imag))
        layer_real = layers[layer][0]
        layer_imag = layers[layer][1]
        mixed_real = wave_real * layer_real - wave_imag * layer_imag
        mixed_imag = wave_real * layer_imag + wave_imag * layer_real
        freq_real, freq_imag = transform(stack(mixed_real, mixed_imag), forward)
        prod_real = freq_real * kernel_real - freq_imag * kernel_imag
        prod_imag = freq_real * kernel_imag + freq_imag * kernel_real
        if layer < sections - 1:
            wave_real, wave_imag = transform(stack(prod_real, prod_imag), inverse)
    far_real, far_imag = prod_real, prod_imag
    residual = far_real * far_real + far_imag * far_imag - measured[0]
    back_real = residual * far_real
    back_imag = residual * far_imag
    pieces = [None] * sections
    for layer in range(sections - 1, -1, -1):
        if layer < sections - 1:
            back_real, back_imag = transform(stack(grad_real, grad_imag), forward)
        prod_real = back_real * kernel_real + back_imag * kernel_imag
        prod_imag = back_imag * kernel_real - back_real * kernel_imag
        inner_real, inner_imag = transform(stack(prod_real, prod_imag), inverse)
        wave_real, wave_imag = saved[layer]
        pieces[layer] = jnp.stack(
            [wave_real * inner_real + wave_imag * inner_imag,
             wave_real * inner_imag - wave_imag * inner_real],
            axis=0,
        )
        if layer > 0:
            layer_real = layers[layer][0]
            layer_imag = layers[layer][1]
            grad_real = layer_real * inner_real + layer_imag * inner_imag
            grad_imag = layer_real * inner_imag - layer_imag * inner_real
    piece = jnp.take(jnp.stack(pieces, axis=0), cut_index, axis=0)

    padded = jnp.concatenate([piece, jnp.zeros_like(piece)], axis=1)
    spill = lax.dynamic_slice(padded, (zero, rows - row, zero), (2, width, width))
    arrived = shifted(spill, "tile", 1)

    own = jnp.pad(piece, ((0, 0), (rows, rows), (columns, columns)))
    own = lax.dynamic_slice(own, (zero, rows - row, columns - column), (2, rows, columns))
    above = jnp.pad(arrived, ((0, 0), (0, rows), (columns, columns)))
    above = lax.dynamic_slice(above, (zero, zero, columns - column_above), (2, rows, columns))
    result = own + above
    return result[None]


def solution(mesh):
    placed = (P("cuts", None, "tile", None), P(), P(), P("tile"), P("tile"), P("tile", None, None))
    return jax.shard_map(
        per_device,
        mesh=mesh,
        in_specs=placed,
        out_specs=P("cuts", None, "tile", None),
        check_vma=False,
    )
```

```python
import jax
import jax.numpy as jnp
from jax import lax
from jax.experimental import pallas as pl
from jax.experimental.pallas import tpu as pltpu
from jax.sharding import PartitionSpec as P


def shifted(value, axis, by):
    devices = lax.axis_size(axis)
    pairs = [(i, i + by) for i in range(devices) if 0 <= i + by < devices]
    return lax.ppermute(value, axis, pairs)


def rotated(value, axis, by):
    devices = lax.axis_size(axis)
    pairs = [(i, (i + by) % devices) for i in range(devices)]
    return lax.ppermute(value, axis, pairs)


def dft_tables(length):
    index = lax.iota(jnp.int32, length)
    product = index[:, None] * index[None, :] % length
    angle = product.astype(jnp.float32) * (2.0 * jnp.pi / length)
    factor = 1.0 / jnp.sqrt(jnp.float32(length))
    return (jnp.cos(angle) * factor, jnp.sin(angle) * factor)


def halves(value):
    scaled = value * jnp.float32(65537.0)
    high = scaled - (scaled - value)
    low = value - high
    return high.astype(jnp.bfloat16), low.astype(jnp.bfloat16)


def stacked_tables(cosines, sines, direction):
    signed = sines * direction
    left = jnp.concatenate(
        [jnp.concatenate([cosines, -signed], axis=1), jnp.concatenate([signed, cosines], axis=1)],
        axis=0,
    )
    right = jnp.concatenate([cosines, signed], axis=1)
    left_high, left_low = halves(left)
    right_high, right_low = halves(right)
    left_split = jnp.concatenate([left_high, left_high, left_low], axis=1)
    right_split = jnp.concatenate([right_high, right_low, right_high], axis=0)
    return left_split, right_split


def split_dot(split_table, value, table_first):
    high, low = halves(value)
    if table_first:
        operand = jnp.concatenate([high, low, high], axis=0)
        return jnp.dot(split_table, operand, preferred_element_type=jnp.float32)
    operand = jnp.concatenate([high, high, low], axis=1)
    return jnp.dot(operand, split_table, preferred_element_type=jnp.float32)


def transform(stacked, tables):
    left, right = tables
    width = right.shape[1] // 2
    middle = split_dot(left, stacked, True)
    products = split_dot(right, middle, False)
    out_real = products[:width, :width] - products[width:, width:]
    out_imag = products[:width, width:] + products[width:, :width]
    return out_real, out_imag


def stack(real_part, imag_part):
    return jnp.concatenate([real_part, imag_part], axis=0)


def exchange_kernel(window_ref, left_ref, right_ref, far_ref, send_sem, recv_sem):
    devices = lax.axis_size("cuts")
    me = lax.axis_index("cuts")
    right = lax.rem(me + 1, devices)
    left = lax.rem(me + devices - 1, devices)
    mesh_ids = pl.DeviceIdType.MESH
    barrier = pltpu.get_barrier_semaphore()
    for neighbour in (left, right):
        pl.semaphore_signal(barrier, inc=1, device_id={"cuts": neighbour}, device_id_type=mesh_ids)
    pl.semaphore_wait(barrier, 2)

    def remote(source, target, slot, neighbour):
        return pltpu.make_async_remote_copy(
            src_ref=source,
            dst_ref=target,
            send_sem=send_sem.at[slot],
            recv_sem=recv_sem.at[slot],
            device_id={"cuts": neighbour},
            device_id_type=mesh_ids,
        )

    passed_left = remote(window_ref.at[0], right_ref.at[0], 0, left)
    passed_right = remote(window_ref.at[1], left_ref.at[1], 1, right)
    passed_left.start()
    passed_right.start()
    passed_left.wait()
    passed_right.wait()
    far_real = remote(right_ref.at[0], far_ref.at[0], 2, left)
    far_imag = remote(left_ref.at[1], far_ref.at[1], 3, right)
    far_real.start()
    far_imag.start()
    kept_left = remote(window_ref.at[1], right_ref.at[1], 4, left)
    kept_right = remote(window_ref.at[0], left_ref.at[0], 5, right)
    kept_left.start()
    kept_right.start()
    far_real.wait()
    far_imag.wait()
    kept_left.wait()
    kept_right.wait()


def exchange(window):
    shape = jax.ShapeDtypeStruct(window.shape, window.dtype)
    vmem = pl.BlockSpec(memory_space=pltpu.VMEM)
    return pl.pallas_call(
        exchange_kernel,
        out_shape=(shape, shape, shape),
        in_specs=[vmem],
        out_specs=(vmem, vmem, vmem),
        scratch_shapes=[pltpu.SemaphoreType.DMA((6,)), pltpu.SemaphoreType.DMA((6,))],
        compiler_params=pltpu.CompilerParams(collective_id=0, has_side_effects=True),
    )(window)


def per_device(transmission, probe, prop_phase, row_off, col_off, measured):
    rows = transmission.shape[2]
    columns = transmission.shape[3]
    width = probe.shape[1]
    sections = lax.axis_size("cuts")
    cut_index = lax.axis_index("cuts")
    cosines, sines = dft_tables(width)
    forward = stacked_tables(cosines, sines, -1.0)
    inverse = stacked_tables(cosines, sines, 1.0)
    kernel_real = jnp.cos(prop_phase)
    kernel_imag = jnp.sin(prop_phase)
    zero = jnp.zeros((), jnp.int32)
    row = row_off[0]
    column = col_off[0]
    offsets_above = shifted(jnp.stack([row, column]), "tile", 1)
    row_above = offsets_above[0]
    column_above = offsets_above[1]

    strip = transmission[0]
    lent = lax.dynamic_slice(strip, (zero, zero, column_above), (2, width, width))
    lent = jnp.pad(lent, ((0, 0), (width, 0), (0, 0)))
    lent = lax.dynamic_slice(lent, (zero, row_above, zero), (2, width, width))
    borrowed = shifted(lent, "tile", -1)
    kept = jnp.pad(strip, ((0, 0), (0, width), (0, 0)))
    kept = lax.dynamic_slice(kept, (zero, row, column), (2, width, width))
    window = kept + borrowed

    if sections == 4:
        from_left, from_right, far = exchange(window)
        have = [window, from_left, far, from_right]
    else:
        have = [window] + [rotated(window, "cuts", k) for k in range(1, sections)]
    layers = [
        lax.select_n((cut_index - layer) % sections, *have) for layer in range(sections)
    ]

    wave_real = probe[0]
    wave_imag = probe[1]
    saved = []
    for layer in range(sections):
        saved.append((wave_real, wave_imag))
        layer_real = layers[layer][0]
        layer_imag = layers[layer][1]
        mixed_real = wave_real * layer_real - wave_imag * layer_imag
        mixed_imag = wave_real * layer_imag + wave_imag * layer_real
        freq_real, freq_imag = transform(stack(mixed_real, mixed_imag), forward)
        prod_real = freq_real * kernel_real - freq_imag * kernel_imag
        prod_imag = freq_real * kernel_imag + freq_imag * kernel_real
        if layer < sections - 1:
            wave_real, wave_imag = transform(stack(prod_real, prod_imag), inverse)
    far_real, far_imag = prod_real, prod_imag
    residual = far_real * far_real + far_imag * far_imag - measured[0]
    back_real = residual * far_real
    back_imag = residual * far_imag
    pieces = [None] * sections
    for layer in range(sections - 1, -1, -1):
        if layer < sections - 1:
            back_real, back_imag = transform(stack(grad_real, grad_imag), forward)
        prod_real = back_real * kernel_real + back_imag * kernel_imag
        prod_imag = back_imag * kernel_real - back_real * kernel_imag
        inner_real, inner_imag = transform(stack(prod_real, prod_imag), inverse)
        wave_real, wave_imag = saved[layer]
        pieces[layer] = jnp.stack(
            [wave_real * inner_real + wave_imag * inner_imag,
             wave_real * inner_imag - wave_imag * inner_real],
            axis=0,
        )
        if layer > 0:
            layer_real = layers[layer][0]
            layer_imag = layers[layer][1]
            grad_real = layer_real * inner_real + layer_imag * inner_imag
            grad_imag = layer_real * inner_imag - layer_imag * inner_real
    piece = jnp.take(jnp.stack(pieces, axis=0), cut_index, axis=0)

    padded = jnp.concatenate([piece, jnp.zeros_like(piece)], axis=1)
    spill = lax.dynamic_slice(padded, (zero, rows - row, zero), (2, width, width))
    arrived = shifted(spill, "tile", 1)

    own = jnp.pad(piece, ((0, 0), (rows, rows), (columns, columns)))
    own = lax.dynamic_slice(own, (zero, rows - row, columns - column), (2, rows, columns))
    above = jnp.pad(arrived, ((0, 0), (0, rows), (columns, columns)))
    above = lax.dynamic_slice(above, (zero, zero, columns - column_above), (2, rows, columns))
    result = own + above
    return result[None]


def solution(mesh):
    placed = (P("cuts", None, "tile", None), P(), P(), P("tile"), P("tile"), P("tile", None, None))
    return jax.shard_map(
        per_device,
        mesh=mesh,
        in_specs=placed,
        out_specs=P("cuts", None, "tile", None),
        check_vma=False,
    )
```

```python
import jax
import jax.numpy as jnp
from jax import lax
from jax.experimental import pallas as pl
from jax.experimental.pallas import tpu as pltpu
from jax.sharding import PartitionSpec as P


def shifted(value, axis, by):
    devices = lax.axis_size(axis)
    pairs = [(i, i + by) for i in range(devices) if 0 <= i + by < devices]
    return lax.ppermute(value, axis, pairs)


def rotated(value, axis, by):
    devices = lax.axis_size(axis)
    pairs = [(i, (i + by) % devices) for i in range(devices)]
    return lax.ppermute(value, axis, pairs)


def dft_tables(length):
    index = lax.iota(jnp.int32, length)
    product = index[:, None] * index[None, :] % length
    angle = product.astype(jnp.float32) * (2.0 * jnp.pi / length)
    factor = 1.0 / jnp.sqrt(jnp.float32(length))
    return (jnp.cos(angle) * factor, jnp.sin(angle) * factor)


def halves(value):
    scaled = value * jnp.float32(65537.0)
    high = scaled - (scaled - value)
    low = value - high
    return high.astype(jnp.bfloat16), low.astype(jnp.bfloat16)


def stacked_tables(cosines, sines, direction):
    signed = sines * direction
    left = jnp.concatenate(
        [jnp.concatenate([cosines, -signed], axis=1), jnp.concatenate([signed, cosines], axis=1)],
        axis=0,
    )
    right = jnp.concatenate([cosines, signed], axis=1)
    left_high, left_low = halves(left)
    right_high, right_low = halves(right)
    return left_high, left_low, right_high, right_low


def stack(real_part, imag_part):
    return jnp.concatenate([real_part, imag_part], axis=0)


def exchange_kernel(window_ref, left_ref, right_ref, far_ref, send_sem, recv_sem):
    devices = lax.axis_size("cuts")
    me = lax.axis_index("cuts")
    right = lax.rem(me + 1, devices)
    left = lax.rem(me + devices - 1, devices)
    mesh_ids = pl.DeviceIdType.MESH
    barrier = pltpu.get_barrier_semaphore()
    for neighbour in (left, right):
        pl.semaphore_signal(barrier, inc=1, device_id={"cuts": neighbour}, device_id_type=mesh_ids)
    pl.semaphore_wait(barrier, 2)

    def remote(source, target, slot, neighbour):
        return pltpu.make_async_remote_copy(
            src_ref=source,
            dst_ref=target,
            send_sem=send_sem.at[slot],
            recv_sem=recv_sem.at[slot],
            device_id={"cuts": neighbour},
            device_id_type=mesh_ids,
        )

    passed_left = remote(window_ref.at[0], right_ref.at[0], 0, left)
    passed_right = remote(window_ref.at[1], left_ref.at[1], 1, right)
    passed_left.start()
    passed_right.start()
    passed_left.wait()
    passed_right.wait()
    far_real = remote(right_ref.at[0], far_ref.at[0], 2, left)
    far_imag = remote(left_ref.at[1], far_ref.at[1], 3, right)
    far_real.start()
    far_imag.start()
    kept_left = remote(window_ref.at[1], right_ref.at[1], 4, left)
    kept_right = remote(window_ref.at[0], left_ref.at[0], 5, right)
    kept_left.start()
    kept_right.start()
    far_real.wait()
    far_imag.wait()
    kept_left.wait()
    kept_right.wait()


def exchange(window):
    shape = jax.ShapeDtypeStruct(window.shape, window.dtype)
    vmem = pl.BlockSpec(memory_space=pltpu.VMEM)
    return pl.pallas_call(
        exchange_kernel,
        out_shape=(shape, shape, shape),
        in_specs=[vmem],
        out_specs=(vmem, vmem, vmem),
        scratch_shapes=[pltpu.SemaphoreType.DMA((6,)), pltpu.SemaphoreType.DMA((6,))],
        compiler_params=pltpu.CompilerParams(collective_id=0, has_side_effects=True),
    )(window)


def kernel_transform(stacked, left_high, left_low, right_high, right_low):
    width = right_high.shape[0]
    high, low = halves(stacked)
    middle = (
        jnp.dot(left_high, high, preferred_element_type=jnp.float32)
        + jnp.dot(left_high, low, preferred_element_type=jnp.float32)
        + jnp.dot(left_low, high, preferred_element_type=jnp.float32)
    )
    high, low = halves(middle)
    products = (
        jnp.dot(high, right_high, preferred_element_type=jnp.float32)
        + jnp.dot(low, right_high, preferred_element_type=jnp.float32)
        + jnp.dot(high, right_low, preferred_element_type=jnp.float32)
    )
    out_real = products[:width, :width] - products[width:, width:]
    out_imag = products[:width, width:] + products[width:, :width]
    return out_real, out_imag


def chain_kernel(probe_ref, layers_ref, kernel_real_ref, kernel_imag_ref, measured_ref,
                 forward_lh, forward_ll, forward_rh, forward_rl,
                 inverse_lh, inverse_ll, inverse_rh, inverse_rl, out_ref):
    sections = layers_ref.shape[0]
    kernel_real = kernel_real_ref[...]
    kernel_imag = kernel_imag_ref[...]

    def forward(value):
        return kernel_transform(value, forward_lh[...], forward_ll[...], forward_rh[...], forward_rl[...])

    def inverse(value):
        return kernel_transform(value, inverse_lh[...], inverse_ll[...], inverse_rh[...], inverse_rl[...])

    wave_real = probe_ref[0]
    wave_imag = probe_ref[1]
    saved = []
    for layer in range(sections):
        saved.append((wave_real, wave_imag))
        layer_real = layers_ref[layer, 0]
        layer_imag = layers_ref[layer, 1]
        mixed_real = wave_real * layer_real - wave_imag * layer_imag
        mixed_imag = wave_real * layer_imag + wave_imag * layer_real
        freq_real, freq_imag = forward(stack(mixed_real, mixed_imag))
        prod_real = freq_real * kernel_real - freq_imag * kernel_imag
        prod_imag = freq_real * kernel_imag + freq_imag * kernel_real
        if layer < sections - 1:
            wave_real, wave_imag = inverse(stack(prod_real, prod_imag))
    far_real, far_imag = prod_real, prod_imag
    residual = far_real * far_real + far_imag * far_imag - measured_ref[...]
    back_real = residual * far_real
    back_imag = residual * far_imag
    for layer in range(sections - 1, -1, -1):
        if layer < sections - 1:
            back_real, back_imag = forward(stack(grad_real, grad_imag))
        prod_real = back_real * kernel_real + back_imag * kernel_imag
        prod_imag = back_imag * kernel_real - back_real * kernel_imag
        inner_real, inner_imag = inverse(stack(prod_real, prod_imag))
        wave_real, wave_imag = saved[layer]
        out_ref[layer, 0] = wave_real * inner_real + wave_imag * inner_imag
        out_ref[layer, 1] = wave_real * inner_imag - wave_imag * inner_real
        if layer > 0:
            layer_real = layers_ref[layer, 0]
            layer_imag = layers_ref[layer, 1]
            grad_real = layer_real * inner_real + layer_imag * inner_imag
            grad_imag = layer_real * inner_imag - layer_imag * inner_real


def run_chain(probe, layers, kernel_real, kernel_imag, measured, forward, inverse):
    vmem = pl.BlockSpec(memory_space=pltpu.VMEM)
    operands = (probe, layers, kernel_real, kernel_imag, measured) + forward + inverse
    return pl.pallas_call(
        chain_kernel,
        out_shape=jax.ShapeDtypeStruct(layers.shape, jnp.float32),
        in_specs=[vmem] * len(operands),
        out_specs=vmem,
        compiler_params=pltpu.CompilerParams(vmem_limit_bytes=48 * 1024 * 1024),
    )(*operands)


def per_device(transmission, probe, prop_phase, row_off, col_off, measured):
    rows = transmission.shape[2]
    columns = transmission.shape[3]
    width = probe.shape[1]
    sections = lax.axis_size("cuts")
    cut_index = lax.axis_index("cuts")
    cosines, sines = dft_tables(width)
    forward = stacked_tables(cosines, sines, -1.0)
    inverse = stacked_tables(cosines, sines, 1.0)
    kernel_real = jnp.cos(prop_phase)
    kernel_imag = jnp.sin(prop_phase)
    zero = jnp.zeros((), jnp.int32)
    row = row_off[0]
    column = col_off[0]
    offsets_above = shifted(jnp.stack([row, column]), "tile", 1)
    row_above = offsets_above[0]
    column_above = offsets_above[1]

    strip = transmission[0]
    lent = lax.dynamic_slice(strip, (zero, zero, column_above), (2, width, width))
    lent = jnp.pad(lent, ((0, 0), (width, 0), (0, 0)))
    lent = lax.dynamic_slice(lent, (zero, row_above, zero), (2, width, width))
    borrowed = shifted(lent, "tile", -1)
    kept = jnp.pad(strip, ((0, 0), (0, width), (0, 0)))
    kept = lax.dynamic_slice(kept, (zero, row, column), (2, width, width))
    window = kept + borrowed

    if sections == 4:
        from_left, from_right, far = exchange(window)
        have = [window, from_left, far, from_right]
    else:
        have = [window] + [rotated(window, "cuts", k) for k in range(1, sections)]
    layers = [
        lax.select_n((cut_index - layer) % sections, *have) for layer in range(sections)
    ]

    pieces = run_chain(
        probe, jnp.stack(layers, axis=0), kernel_real, kernel_imag, measured[0], forward, inverse
    )
    piece = jnp.take(pieces, cut_index, axis=0)

    padded = jnp.concatenate([piece, jnp.zeros_like(piece)], axis=1)
    spill = lax.dynamic_slice(padded, (zero, rows - row, zero), (2, width, width))
    arrived = shifted(spill, "tile", 1)

    own = jnp.pad(piece, ((0, 0), (rows, rows), (columns, columns)))
    own = lax.dynamic_slice(own, (zero, rows - row, columns - column), (2, rows, columns))
    above = jnp.pad(arrived, ((0, 0), (0, rows), (columns, columns)))
    above = lax.dynamic_slice(above, (zero, zero, columns - column_above), (2, rows, columns))
    result = own + above
    return result[None]


def solution(mesh):
    placed = (P("cuts", None, "tile", None), P(), P(), P("tile"), P("tile"), P("tile", None, None))
    return jax.shard_map(
        per_device,
        mesh=mesh,
        in_specs=placed,
        out_specs=P("cuts", None, "tile", None),
        check_vma=False,
    )
```

```python
import jax
import jax.numpy as jnp
from jax import lax
from jax.experimental import pallas as pl
from jax.experimental.pallas import tpu as pltpu
from jax.sharding import PartitionSpec as P


def shifted(value, axis, by):
    devices = lax.axis_size(axis)
    pairs = [(i, i + by) for i in range(devices) if 0 <= i + by < devices]
    return lax.ppermute(value, axis, pairs)


def rotated(value, axis, by):
    devices = lax.axis_size(axis)
    pairs = [(i, (i + by) % devices) for i in range(devices)]
    return lax.ppermute(value, axis, pairs)


def dft_tables(length):
    index = lax.iota(jnp.int32, length)
    product = index[:, None] * index[None, :] % length
    angle = product.astype(jnp.float32) * (2.0 * jnp.pi / length)
    factor = 1.0 / jnp.sqrt(jnp.float32(length))
    return (jnp.cos(angle) * factor, jnp.sin(angle) * factor)


def halves(value):
    scaled = value * jnp.float32(65537.0)
    high = scaled - (scaled - value)
    low = value - high
    return high.astype(jnp.bfloat16), low.astype(jnp.bfloat16)


def stacked_tables(cosines, sines, direction):
    signed = sines * direction
    left = jnp.concatenate(
        [jnp.concatenate([cosines, -signed], axis=1), jnp.concatenate([signed, cosines], axis=1)],
        axis=0,
    )
    right = jnp.concatenate([cosines, signed], axis=1)
    left_high, left_low = halves(left)
    right_high, right_low = halves(right)
    left_split = jnp.concatenate([left_high, left_high, left_low], axis=1)
    right_split = jnp.concatenate([right_high, right_low, right_high], axis=0)
    return left_split, right_split


def split_dot(split_table, value, table_first):
    high, low = halves(value)
    if table_first:
        operand = jnp.concatenate([high, low, high], axis=0)
        return jnp.dot(split_table, operand, preferred_element_type=jnp.float32)
    operand = jnp.concatenate([high, high, low], axis=1)
    return jnp.dot(operand, split_table, preferred_element_type=jnp.float32)


def transform(stacked, tables):
    left, right = tables
    width = right.shape[1] // 2
    middle = split_dot(left, stacked, True)
    products = split_dot(right, middle, False)
    out_real = products[:width, :width] - products[width:, width:]
    out_imag = products[:width, width:] + products[width:, :width]
    return out_real, out_imag


def stack(real_part, imag_part):
    return jnp.concatenate([real_part, imag_part], axis=0)


def exchange_kernel(window_ref, left_ref, right_ref, far_ref, send_sem, recv_sem):
    devices = lax.axis_size("cuts")
    me = lax.axis_index("cuts")
    right = lax.rem(me + 1, devices)
    left = lax.rem(me + devices - 1, devices)
    mesh_ids = pl.DeviceIdType.MESH
    barrier = pltpu.get_barrier_semaphore()
    for neighbour in (left, right):
        pl.semaphore_signal(barrier, inc=1, device_id={"cuts": neighbour}, device_id_type=mesh_ids)
    pl.semaphore_wait(barrier, 2)

    def remote(source, target, slot, neighbour):
        return pltpu.make_async_remote_copy(
            src_ref=source,
            dst_ref=target,
            send_sem=send_sem.at[slot],
            recv_sem=recv_sem.at[slot],
            device_id={"cuts": neighbour},
            device_id_type=mesh_ids,
        )

    passed_left = remote(window_ref.at[0], right_ref.at[0], 0, left)
    passed_right = remote(window_ref.at[1], left_ref.at[1], 1, right)
    passed_left.start()
    passed_right.start()
    passed_left.wait()
    passed_right.wait()
    far_real = remote(right_ref.at[0], far_ref.at[0], 2, left)
    far_imag = remote(left_ref.at[1], far_ref.at[1], 3, right)
    far_real.start()
    far_imag.start()
    kept_left = remote(window_ref.at[1], right_ref.at[1], 4, left)
    kept_right = remote(window_ref.at[0], left_ref.at[0], 5, right)
    kept_left.start()
    kept_right.start()
    far_real.wait()
    far_imag.wait()
    kept_left.wait()
    kept_right.wait()


def exchange(window):
    shape = jax.ShapeDtypeStruct(window.shape, window.dtype)
    vmem = pl.BlockSpec(memory_space=pltpu.VMEM)
    return pl.pallas_call(
        exchange_kernel,
        out_shape=(shape, shape, shape),
        in_specs=[vmem],
        out_specs=(vmem, vmem, vmem),
        scratch_shapes=[pltpu.SemaphoreType.DMA((6,)), pltpu.SemaphoreType.DMA((6,))],
        compiler_params=pltpu.CompilerParams(collective_id=0, has_side_effects=True),
    )(window)


def per_device(transmission, probe, prop_phase, row_off, col_off, measured):
    rows = transmission.shape[2]
    columns = transmission.shape[3]
    width = probe.shape[1]
    sections = lax.axis_size("cuts")
    cut_index = lax.axis_index("cuts")
    cosines, sines = dft_tables(width)
    forward = stacked_tables(cosines, sines, -1.0)
    inverse = stacked_tables(cosines, sines, 1.0)
    kernel_real = jnp.cos(prop_phase)
    kernel_imag = jnp.sin(prop_phase)
    zero = jnp.zeros((), jnp.int32)
    row = row_off[0]
    column = col_off[0]
    offsets_above = shifted(jnp.stack([row, column]), "tile", 1)
    row_above = offsets_above[0]
    column_above = offsets_above[1]

    strip = transmission[0]
    lent = lax.dynamic_slice(strip, (zero, zero, column_above), (2, width, width))
    lent = jnp.pad(lent, ((0, 0), (width, 0), (0, 0)))
    lent = lax.dynamic_slice(lent, (zero, row_above, zero), (2, width, width))
    borrowed = shifted(lent, "tile", -1)
    kept = jnp.pad(strip, ((0, 0), (0, width), (0, 0)))
    kept = lax.dynamic_slice(kept, (zero, row, column), (2, width, width))
    window = kept + borrowed

    if sections == 4:
        from_left, from_right, far = exchange(window)
        have = [window, from_left, far, from_right]
    else:
        have = [window] + [rotated(window, "cuts", k) for k in range(1, sections)]
    layers = [
        lax.select_n((cut_index - layer) % sections, *have) for layer in range(sections)
    ]

    wave_real = probe[0]
    wave_imag = probe[1]
    saved = []
    for layer in range(sections):
        saved.append((wave_real, wave_imag))
        layer_real = layers[layer][0]
        layer_imag = layers[layer][1]
        mixed_real = wave_real * layer_real - wave_imag * layer_imag
        mixed_imag = wave_real * layer_imag + wave_imag * layer_real
        freq_real, freq_imag = transform(stack(mixed_real, mixed_imag), forward)
        prod_real = freq_real * kernel_real - freq_imag * kernel_imag
        prod_imag = freq_real * kernel_imag + freq_imag * kernel_real
        if layer < sections - 1:
            wave_real, wave_imag = transform(stack(prod_real, prod_imag), inverse)
    far_real, far_imag = prod_real, prod_imag
    residual = far_real * far_real + far_imag * far_imag - measured[0]
    back_real = residual * far_real
    back_imag = residual * far_imag
    pieces = [None] * sections
    for layer in range(sections - 1, -1, -1):
        if layer < sections - 1:
            back_real, back_imag = transform(stack(grad_real, grad_imag), forward)
        prod_real = back_real * kernel_real + back_imag * kernel_imag
        prod_imag = back_imag * kernel_real - back_real * kernel_imag
        inner_real, inner_imag = transform(stack(prod_real, prod_imag), inverse)
        wave_real, wave_imag = saved[layer]
        pieces[layer] = jnp.stack(
            [wave_real * inner_real + wave_imag * inner_imag,
             wave_real * inner_imag - wave_imag * inner_real],
            axis=0,
        )
        if layer > 0:
            layer_real = layers[layer][0]
            layer_imag = layers[layer][1]
            grad_real = layer_real * inner_real + layer_imag * inner_imag
            grad_imag = layer_real * inner_imag - layer_imag * inner_real
    piece = jnp.take(jnp.stack(pieces, axis=0), cut_index, axis=0)

    padded = jnp.concatenate([piece, jnp.zeros_like(piece)], axis=1)
    spill = lax.dynamic_slice(padded, (zero, rows - row, zero), (2, width, width))
    arrived = shifted(spill, "tile", 1)

    own = jnp.pad(piece, ((0, 0), (rows, rows), (columns, columns)))
    own = lax.dynamic_slice(own, (zero, rows - row, columns - column), (2, rows, columns))
    current = lax.dynamic_slice(own, (zero, zero, column_above), (2, width, width))
    result = lax.dynamic_update_slice(own, current + arrived, (zero, zero, column_above))
    return result[None]


def solution(mesh):
    placed = (P("cuts", None, "tile", None), P(), P(), P("tile"), P("tile"), P("tile", None, None))
    return jax.shard_map(
        per_device,
        mesh=mesh,
        in_specs=placed,
        out_specs=P("cuts", None, "tile", None),
        check_vma=False,
    )
```

```python
import jax
import jax.numpy as jnp
from jax import lax
from jax.experimental import pallas as pl
from jax.experimental.pallas import tpu as pltpu
from jax.sharding import PartitionSpec as P


def shifted(value, axis, by):
    devices = lax.axis_size(axis)
    pairs = [(i, i + by) for i in range(devices) if 0 <= i + by < devices]
    return lax.ppermute(value, axis, pairs)


def rotated(value, axis, by):
    devices = lax.axis_size(axis)
    pairs = [(i, (i + by) % devices) for i in range(devices)]
    return lax.ppermute(value, axis, pairs)


def dft_tables(length):
    index = lax.iota(jnp.int32, length)
    product = index[:, None] * index[None, :] % length
    angle = product.astype(jnp.float32) * (2.0 * jnp.pi / length)
    factor = 1.0 / jnp.sqrt(jnp.float32(length))
    return (jnp.cos(angle) * factor, jnp.sin(angle) * factor)


def halves(value):
    scaled = value * jnp.float32(65537.0)
    high = scaled - (scaled - value)
    low = value - high
    return high.astype(jnp.bfloat16), low.astype(jnp.bfloat16)


def stacked_tables(cosines, sines, direction):
    signed = sines * direction
    left = jnp.concatenate(
        [jnp.concatenate([cosines, -signed], axis=1), jnp.concatenate([signed, cosines], axis=1)],
        axis=0,
    )
    right = jnp.concatenate([cosines, signed], axis=1)
    left_high, left_low = halves(left)
    right_high, right_low = halves(right)
    left_split = jnp.concatenate([left_high, left_high, left_low], axis=1)
    right_split = jnp.concatenate([right_high, right_low, right_high], axis=0)
    return left_split, right_split


def split_dot(split_table, value, table_first):
    high, low = halves(value)
    if table_first:
        operand = jnp.concatenate([high, low, high], axis=0)
        return jnp.dot(split_table, operand, preferred_element_type=jnp.float32)
    operand = jnp.concatenate([high, high, low], axis=1)
    return jnp.dot(operand, split_table, preferred_element_type=jnp.float32)


def transform(stacked, tables):
    left, right = tables
    width = right.shape[1] // 2
    middle = split_dot(left, stacked, True)
    products = split_dot(right, middle, False)
    out_real = products[:width, :width] - products[width:, width:]
    out_imag = products[:width, width:] + products[width:, :width]
    return out_real, out_imag


def stack(real_part, imag_part):
    return jnp.concatenate([real_part, imag_part], axis=0)


def exchange_kernel(window_ref, layers_ref, send_sem, recv_sem):
    devices = lax.axis_size("cuts")
    me = lax.axis_index("cuts")
    right = lax.rem(me + 1, devices)
    left = lax.rem(me + devices - 1, devices)
    mesh_ids = pl.DeviceIdType.MESH
    barrier = pltpu.get_barrier_semaphore()
    for neighbour in (left, right):
        pl.semaphore_signal(barrier, inc=1, device_id={"cuts": neighbour}, device_id_type=mesh_ids)
    pl.semaphore_wait(barrier, 2)

    def remote(source, target, slot, neighbour):
        return pltpu.make_async_remote_copy(
            src_ref=source,
            dst_ref=target,
            send_sem=send_sem.at[slot],
            recv_sem=recv_sem.at[slot],
            device_id={"cuts": neighbour},
            device_id_type=mesh_ids,
        )

    passed_left = remote(window_ref.at[0], layers_ref.at[me, 0], 0, left)
    passed_right = remote(window_ref.at[1], layers_ref.at[me, 1], 1, right)
    passed_left.start()
    passed_right.start()
    layers_ref[me] = window_ref[...]
    passed_left.wait()
    passed_right.wait()
    far_real = remote(layers_ref.at[right, 0], layers_ref.at[right, 0], 2, left)
    far_imag = remote(layers_ref.at[left, 1], layers_ref.at[left, 1], 3, right)
    far_real.start()
    far_imag.start()
    kept_left = remote(window_ref.at[1], layers_ref.at[me, 1], 4, left)
    kept_right = remote(window_ref.at[0], layers_ref.at[me, 0], 5, right)
    kept_left.start()
    kept_right.start()
    far_real.wait()
    far_imag.wait()
    kept_left.wait()
    kept_right.wait()


def exchange(window, sections):
    shape = jax.ShapeDtypeStruct((sections,) + window.shape, window.dtype)
    vmem = pl.BlockSpec(memory_space=pltpu.VMEM)
    return pl.pallas_call(
        exchange_kernel,
        out_shape=shape,
        in_specs=[vmem],
        out_specs=vmem,
        scratch_shapes=[pltpu.SemaphoreType.DMA((6,)), pltpu.SemaphoreType.DMA((6,))],
        compiler_params=pltpu.CompilerParams(collective_id=0, has_side_effects=True),
    )(window)


def per_device(transmission, probe, prop_phase, row_off, col_off, measured):
    rows = transmission.shape[2]
    columns = transmission.shape[3]
    width = probe.shape[1]
    sections = lax.axis_size("cuts")
    cut_index = lax.axis_index("cuts")
    cosines, sines = dft_tables(width)
    forward = stacked_tables(cosines, sines, -1.0)
    inverse = stacked_tables(cosines, sines, 1.0)
    kernel_real = jnp.cos(prop_phase)
    kernel_imag = jnp.sin(prop_phase)
    zero = jnp.zeros((), jnp.int32)
    row = row_off[0]
    column = col_off[0]
    offsets_above = shifted(jnp.stack([row, column]), "tile", 1)
    row_above = offsets_above[0]
    column_above = offsets_above[1]

    strip = transmission[0]
    lent = lax.dynamic_slice(strip, (zero, zero, column_above), (2, width, width))
    lent = jnp.pad(lent, ((0, 0), (width, 0), (0, 0)))
    lent = lax.dynamic_slice(lent, (zero, row_above, zero), (2, width, width))
    borrowed = shifted(lent, "tile", -1)
    kept = jnp.pad(strip, ((0, 0), (0, width), (0, 0)))
    kept = lax.dynamic_slice(kept, (zero, row, column), (2, width, width))
    window = kept + borrowed

    if sections == 4:
        stacked_layers = exchange(window, sections)
        layers = [stacked_layers[layer] for layer in range(sections)]
    else:
        have = [window] + [rotated(window, "cuts", k) for k in range(1, sections)]
        layers = [
            lax.select_n((cut_index - layer) % sections, *have) for layer in range(sections)
        ]

    wave_real = probe[0]
    wave_imag = probe[1]
    saved = []
    for layer in range(sections):
        saved.append((wave_real, wave_imag))
        layer_real = layers[layer][0]
        layer_imag = layers[layer][1]
        mixed_real = wave_real * layer_real - wave_imag * layer_imag
        mixed_imag = wave_real * layer_imag + wave_imag * layer_real
        freq_real, freq_imag = transform(stack(mixed_real, mixed_imag), forward)
        prod_real = freq_real * kernel_real - freq_imag * kernel_imag
        prod_imag = freq_real * kernel_imag + freq_imag * kernel_real
        if layer < sections - 1:
            wave_real, wave_imag = transform(stack(prod_real, prod_imag), inverse)
    far_real, far_imag = prod_real, prod_imag
    residual = far_real * far_real + far_imag * far_imag - measured[0]
    back_real = residual * far_real
    back_imag = residual * far_imag
    pieces = [None] * sections
    for layer in range(sections - 1, -1, -1):
        if layer < sections - 1:
            back_real, back_imag = transform(stack(grad_real, grad_imag), forward)
        prod_real = back_real * kernel_real + back_imag * kernel_imag
        prod_imag = back_imag * kernel_real - back_real * kernel_imag
        inner_real, inner_imag = transform(stack(prod_real, prod_imag), inverse)
        wave_real, wave_imag = saved[layer]
        pieces[layer] = jnp.stack(
            [wave_real * inner_real + wave_imag * inner_imag,
             wave_real * inner_imag - wave_imag * inner_real],
            axis=0,
        )
        if layer > 0:
            layer_real = layers[layer][0]
            layer_imag = layers[layer][1]
            grad_real = layer_real * inner_real + layer_imag * inner_imag
            grad_imag = layer_real * inner_imag - layer_imag * inner_real
    piece = jnp.take(jnp.stack(pieces, axis=0), cut_index, axis=0)

    padded = jnp.concatenate([piece, jnp.zeros_like(piece)], axis=1)
    spill = lax.dynamic_slice(padded, (zero, rows - row, zero), (2, width, width))
    arrived = shifted(spill, "tile", 1)

    own = jnp.pad(piece, ((0, 0), (rows, rows), (columns, columns)))
    own = lax.dynamic_slice(own, (zero, rows - row, columns - column), (2, rows, columns))
    above = jnp.pad(arrived, ((0, 0), (0, rows), (columns, columns)))
    above = lax.dynamic_slice(above, (zero, zero, columns - column_above), (2, rows, columns))
    result = own + above
    return result[None]


def solution(mesh):
    placed = (P("cuts", None, "tile", None), P(), P(), P("tile"), P("tile"), P("tile", None, None))
    return jax.shard_map(
        per_device,
        mesh=mesh,
        in_specs=placed,
        out_specs=P("cuts", None, "tile", None),
        check_vma=False,
    )
```

```python
import jax
import jax.numpy as jnp
from jax import lax
from jax.experimental import pallas as pl
from jax.experimental.pallas import tpu as pltpu
from jax.sharding import PartitionSpec as P


def shifted(value, axis, by):
    devices = lax.axis_size(axis)
    pairs = [(i, i + by) for i in range(devices) if 0 <= i + by < devices]
    return lax.ppermute(value, axis, pairs)


def rotated(value, axis, by):
    devices = lax.axis_size(axis)
    pairs = [(i, (i + by) % devices) for i in range(devices)]
    return lax.ppermute(value, axis, pairs)


def dft_tables(length):
    index = lax.iota(jnp.int32, length)
    product = index[:, None] * index[None, :] % length
    angle = product.astype(jnp.float32) * (2.0 * jnp.pi / length)
    factor = 1.0 / jnp.sqrt(jnp.float32(length))
    return (jnp.cos(angle) * factor, jnp.sin(angle) * factor)


def halves(value):
    scaled = value * jnp.float32(65537.0)
    high = scaled - (scaled - value)
    low = value - high
    return high.astype(jnp.bfloat16), low.astype(jnp.bfloat16)


def stacked_tables(cosines, sines, direction):
    signed = sines * direction
    left = jnp.concatenate(
        [jnp.concatenate([cosines, -signed], axis=1), jnp.concatenate([signed, cosines], axis=1)],
        axis=0,
    )
    right = jnp.concatenate([cosines, signed], axis=1)
    left_high, left_low = halves(left)
    right_high, right_low = halves(right)
    left_split = jnp.concatenate([left_high, left_high, left_low], axis=1)
    right_split = jnp.concatenate([right_high, right_low, right_high], axis=0)
    return left_split, right_split


def split_dot(split_table, value, table_first):
    high, low = halves(value)
    if table_first:
        operand = jnp.concatenate([high, low, high], axis=0)
        return jnp.dot(split_table, operand, preferred_element_type=jnp.float32)
    operand = jnp.concatenate([high, high, low], axis=1)
    return jnp.dot(operand, split_table, preferred_element_type=jnp.float32)


def transform(stacked, tables):
    left, right = tables
    width = right.shape[1] // 2
    middle = split_dot(left, stacked, True)
    products = split_dot(right, middle, False)
    out_real = products[:width, :width] - products[width:, width:]
    out_imag = products[:width, width:] + products[width:, :width]
    return out_real, out_imag


def stack(real_part, imag_part):
    return jnp.concatenate([real_part, imag_part], axis=0)


def exchange_kernel(window_ref, layers_ref, send_sem, recv_sem):
    devices = lax.axis_size("cuts")
    me = lax.axis_index("cuts")
    right = lax.rem(me + 1, devices)
    left = lax.rem(me + devices - 1, devices)
    mesh_ids = pl.DeviceIdType.MESH
    barrier = pltpu.get_barrier_semaphore()
    for neighbour in (left, right):
        pl.semaphore_signal(barrier, inc=1, device_id={"cuts": neighbour}, device_id_type=mesh_ids)
    pl.semaphore_wait(barrier, 2)

    rows = window_ref.shape[1]
    half = rows // 2

    def remote(source, target, slot, neighbour):
        return [
            pltpu.make_async_remote_copy(
                src_ref=source.at[pl.ds(part * half, half)],
                dst_ref=target.at[pl.ds(part * half, half)],
                send_sem=send_sem.at[2 * slot + part],
                recv_sem=recv_sem.at[2 * slot + part],
                device_id={"cuts": neighbour},
                device_id_type=mesh_ids,
            )
            for part in range(2)
        ]

    def start(copies):
        for copy in copies:
            copy.start()

    def wait(copies):
        for copy in copies:
            copy.wait()

    passed_left = remote(window_ref.at[0], layers_ref.at[me, 0], 0, left)
    passed_right = remote(window_ref.at[1], layers_ref.at[me, 1], 1, right)
    start(passed_left)
    start(passed_right)
    layers_ref[me] = window_ref[...]
    wait(passed_left)
    wait(passed_right)
    far_real = remote(layers_ref.at[right, 0], layers_ref.at[right, 0], 2, left)
    far_imag = remote(layers_ref.at[left, 1], layers_ref.at[left, 1], 3, right)
    start(far_real)
    start(far_imag)
    kept_left = remote(window_ref.at[1], layers_ref.at[me, 1], 4, left)
    kept_right = remote(window_ref.at[0], layers_ref.at[me, 0], 5, right)
    start(kept_left)
    start(kept_right)
    wait(far_real)
    wait(far_imag)
    wait(kept_left)
    wait(kept_right)


def exchange(window, sections):
    shape = jax.ShapeDtypeStruct((sections,) + window.shape, window.dtype)
    vmem = pl.BlockSpec(memory_space=pltpu.VMEM)
    return pl.pallas_call(
        exchange_kernel,
        out_shape=shape,
        in_specs=[vmem],
        out_specs=vmem,
        scratch_shapes=[pltpu.SemaphoreType.DMA((12,)), pltpu.SemaphoreType.DMA((12,))],
        compiler_params=pltpu.CompilerParams(collective_id=0, has_side_effects=True),
    )(window)


def per_device(transmission, probe, prop_phase, row_off, col_off, measured):
    rows = transmission.shape[2]
    columns = transmission.shape[3]
    width = probe.shape[1]
    sections = lax.axis_size("cuts")
    cut_index = lax.axis_index("cuts")
    cosines, sines = dft_tables(width)
    forward = stacked_tables(cosines, sines, -1.0)
    inverse = stacked_tables(cosines, sines, 1.0)
    kernel_real = jnp.cos(prop_phase)
    kernel_imag = jnp.sin(prop_phase)
    zero = jnp.zeros((), jnp.int32)
    row = row_off[0]
    column = col_off[0]
    offsets_above = shifted(jnp.stack([row, column]), "tile", 1)
    row_above = offsets_above[0]
    column_above = offsets_above[1]

    strip = transmission[0]
    lent = lax.dynamic_slice(strip, (zero, zero, column_above), (2, width, width))
    lent = jnp.pad(lent, ((0, 0), (width, 0), (0, 0)))
    lent = lax.dynamic_slice(lent, (zero, row_above, zero), (2, width, width))
    borrowed = shifted(lent, "tile", -1)
    kept = jnp.pad(strip, ((0, 0), (0, width), (0, 0)))
    kept = lax.dynamic_slice(kept, (zero, row, column), (2, width, width))
    window = kept + borrowed

    if sections == 4:
        stacked_layers = exchange(window, sections)
        layers = [stacked_layers[layer] for layer in range(sections)]
    else:
        have = [window] + [rotated(window, "cuts", k) for k in range(1, sections)]
        layers = [
            lax.select_n((cut_index - layer) % sections, *have) for layer in range(sections)
        ]

    wave_real = probe[0]
    wave_imag = probe[1]
    saved = []
    for layer in range(sections):
        saved.append((wave_real, wave_imag))
        layer_real = layers[layer][0]
        layer_imag = layers[layer][1]
        mixed_real = wave_real * layer_real - wave_imag * layer_imag
        mixed_imag = wave_real * layer_imag + wave_imag * layer_real
        freq_real, freq_imag = transform(stack(mixed_real, mixed_imag), forward)
        prod_real = freq_real * kernel_real - freq_imag * kernel_imag
        prod_imag = freq_real * kernel_imag + freq_imag * kernel_real
        if layer < sections - 1:
            wave_real, wave_imag = transform(stack(prod_real, prod_imag), inverse)
    far_real, far_imag = prod_real, prod_imag
    residual = far_real * far_real + far_imag * far_imag - measured[0]
    back_real = residual * far_real
    back_imag = residual * far_imag
    pieces = [None] * sections
    for layer in range(sections - 1, -1, -1):
        if layer < sections - 1:
            back_real, back_imag = transform(stack(grad_real, grad_imag), forward)
        prod_real = back_real * kernel_real + back_imag * kernel_imag
        prod_imag = back_imag * kernel_real - back_real * kernel_imag
        inner_real, inner_imag = transform(stack(prod_real, prod_imag), inverse)
        wave_real, wave_imag = saved[layer]
        pieces[layer] = jnp.stack(
            [wave_real * inner_real + wave_imag * inner_imag,
             wave_real * inner_imag - wave_imag * inner_real],
            axis=0,
        )
        if layer > 0:
            layer_real = layers[layer][0]
            layer_imag = layers[layer][1]
            grad_real = layer_real * inner_real + layer_imag * inner_imag
            grad_imag = layer_real * inner_imag - layer_imag * inner_real
    piece = jnp.take(jnp.stack(pieces, axis=0), cut_index, axis=0)

    padded = jnp.concatenate([piece, jnp.zeros_like(piece)], axis=1)
    spill = lax.dynamic_slice(padded, (zero, rows - row, zero), (2, width, width))
    arrived = shifted(spill, "tile", 1)

    own = jnp.pad(piece, ((0, 0), (rows, rows), (columns, columns)))
    own = lax.dynamic_slice(own, (zero, rows - row, columns - column), (2, rows, columns))
    above = jnp.pad(arrived, ((0, 0), (0, rows), (columns, columns)))
    above = lax.dynamic_slice(above, (zero, zero, columns - column_above), (2, rows, columns))
    result = own + above
    return result[None]


def solution(mesh):
    placed = (P("cuts", None, "tile", None), P(), P(), P("tile"), P("tile"), P("tile", None, None))
    return jax.shard_map(
        per_device,
        mesh=mesh,
        in_specs=placed,
        out_specs=P("cuts", None, "tile", None),
        check_vma=False,
    )
```

```python
import jax
import jax.numpy as jnp
from jax import lax
from jax.experimental import pallas as pl
from jax.experimental.pallas import tpu as pltpu
from jax.sharding import PartitionSpec as P


def shifted(value, axis, by):
    devices = lax.axis_size(axis)
    pairs = [(i, i + by) for i in range(devices) if 0 <= i + by < devices]
    return lax.ppermute(value, axis, pairs)


def rotated(value, axis, by):
    devices = lax.axis_size(axis)
    pairs = [(i, (i + by) % devices) for i in range(devices)]
    return lax.ppermute(value, axis, pairs)


def dft_tables(length):
    index = lax.iota(jnp.int32, length)
    product = index[:, None] * index[None, :] % length
    angle = product.astype(jnp.float32) * (2.0 * jnp.pi / length)
    factor = 1.0 / jnp.sqrt(jnp.float32(length))
    return (jnp.cos(angle) * factor, jnp.sin(angle) * factor)


def halves(value):
    scaled = value * jnp.float32(65537.0)
    high = scaled - (scaled - value)
    low = value - high
    return high.astype(jnp.bfloat16), low.astype(jnp.bfloat16)


def stacked_tables(cosines, sines, direction):
    signed = sines * direction
    left = jnp.concatenate(
        [jnp.concatenate([cosines, -signed], axis=1), jnp.concatenate([signed, cosines], axis=1)],
        axis=0,
    )
    right = jnp.concatenate([cosines, signed], axis=1)
    left_high, left_low = halves(left)
    right_high, right_low = halves(right)
    left_split = jnp.concatenate([left_high, left_high, left_low], axis=1)
    right_split = jnp.concatenate([right_high, right_low, right_high], axis=0)
    return left_split, right_split


def split_dot(split_table, value, table_first):
    high, low = halves(value)
    if table_first:
        operand = jnp.concatenate([high, low, high], axis=0)
        return jnp.dot(split_table, operand, preferred_element_type=jnp.float32)
    operand = jnp.concatenate([high, high, low], axis=1)
    return jnp.dot(operand, split_table, preferred_element_type=jnp.float32)


def transform(stacked, tables):
    left, right = tables
    width = right.shape[1] // 2
    middle = split_dot(left, stacked, True)
    products = split_dot(right, middle, False)
    out_real = products[:width, :width] - products[width:, width:]
    out_imag = products[:width, width:] + products[width:, :width]
    return out_real, out_imag


def stack(real_part, imag_part):
    return jnp.concatenate([real_part, imag_part], axis=0)


def exchange_kernel(window_ref, layers_ref, send_sem, recv_sem):
    devices = lax.axis_size("cuts")
    me = lax.axis_index("cuts")
    right = lax.rem(me + 1, devices)
    left = lax.rem(me + devices - 1, devices)
    mesh_ids = pl.DeviceIdType.MESH
    barrier = pltpu.get_barrier_semaphore()
    for neighbour in (left, right):
        pl.semaphore_signal(barrier, inc=1, device_id={"cuts": neighbour}, device_id_type=mesh_ids)
    pl.semaphore_wait(barrier, 2)

    def remote(source, target, slot, neighbour):
        return pltpu.make_async_remote_copy(
            src_ref=source,
            dst_ref=target,
            send_sem=send_sem.at[slot],
            recv_sem=recv_sem.at[slot],
            device_id={"cuts": neighbour},
            device_id_type=mesh_ids,
        )

    passed_left = remote(window_ref.at[0], layers_ref.at[me, 0], 0, left)
    passed_right = remote(window_ref.at[1], layers_ref.at[me, 1], 1, right)
    passed_left.start()
    passed_right.start()
    layers_ref[me] = window_ref[...]
    passed_left.wait()
    passed_right.wait()
    far_real = remote(layers_ref.at[right, 0], layers_ref.at[right, 0], 2, left)
    far_imag = remote(layers_ref.at[left, 1], layers_ref.at[left, 1], 3, right)
    far_real.start()
    far_imag.start()
    kept_left = remote(window_ref.at[1], layers_ref.at[me, 1], 4, left)
    kept_right = remote(window_ref.at[0], layers_ref.at[me, 0], 5, right)
    kept_left.start()
    kept_right.start()
    far_real.wait()
    far_imag.wait()
    kept_left.wait()
    kept_right.wait()


def exchange(window, sections):
    shape = jax.ShapeDtypeStruct((sections,) + window.shape, window.dtype)
    vmem = pl.BlockSpec(memory_space=pltpu.VMEM)
    return pl.pallas_call(
        exchange_kernel,
        out_shape=shape,
        in_specs=[vmem],
        out_specs=vmem,
        scratch_shapes=[pltpu.SemaphoreType.DMA((6,)), pltpu.SemaphoreType.DMA((6,))],
        compiler_params=pltpu.CompilerParams(collective_id=0, has_side_effects=True),
    )(window)


def per_device(transmission, probe, prop_phase, row_off, col_off, measured):
    rows = transmission.shape[2]
    columns = transmission.shape[3]
    width = probe.shape[1]
    sections = lax.axis_size("cuts")
    cut_index = lax.axis_index("cuts")
    cosines, sines = dft_tables(width)
    forward = stacked_tables(cosines, sines, -1.0)
    inverse = stacked_tables(cosines, sines, 1.0)
    kernel_real = jnp.cos(prop_phase)
    kernel_imag = jnp.sin(prop_phase)
    zero = jnp.zeros((), jnp.int32)
    row = row_off[0]
    column = col_off[0]
    offsets_above = shifted(jnp.stack([row, column]), "tile", 1)
    row_above = offsets_above[0]
    column_above = offsets_above[1]

    strip = transmission[0]
    lent = lax.dynamic_slice(strip, (zero, zero, column_above), (2, width, width))
    lent = jnp.pad(lent, ((0, 0), (width, 0), (0, 0)))
    lent = lax.dynamic_slice(lent, (zero, row_above, zero), (2, width, width))
    borrowed = jnp.stack([shifted(lent[0], "tile", -1), shifted(lent[1], "tile", -1)], axis=0)
    kept = jnp.pad(strip, ((0, 0), (0, width), (0, 0)))
    kept = lax.dynamic_slice(kept, (zero, row, column), (2, width, width))
    window = kept + borrowed

    if sections == 4:
        stacked_layers = exchange(window, sections)
        layers = [stacked_layers[layer] for layer in range(sections)]
    else:
        have = [window] + [rotated(window, "cuts", k) for k in range(1, sections)]
        layers = [
            lax.select_n((cut_index - layer) % sections, *have) for layer in range(sections)
        ]

    wave_real = probe[0]
    wave_imag = probe[1]
    saved = []
    for layer in range(sections):
        saved.append((wave_real, wave_imag))
        layer_real = layers[layer][0]
        layer_imag = layers[layer][1]
        mixed_real = wave_real * layer_real - wave_imag * layer_imag
        mixed_imag = wave_real * layer_imag + wave_imag * layer_real
        freq_real, freq_imag = transform(stack(mixed_real, mixed_imag), forward)
        prod_real = freq_real * kernel_real - freq_imag * kernel_imag
        prod_imag = freq_real * kernel_imag + freq_imag * kernel_real
        if layer < sections - 1:
            wave_real, wave_imag = transform(stack(prod_real, prod_imag), inverse)
    far_real, far_imag = prod_real, prod_imag
    residual = far_real * far_real + far_imag * far_imag - measured[0]
    back_real = residual * far_real
    back_imag = residual * far_imag
    pieces = [None] * sections
    for layer in range(sections - 1, -1, -1):
        if layer < sections - 1:
            back_real, back_imag = transform(stack(grad_real, grad_imag), forward)
        prod_real = back_real * kernel_real + back_imag * kernel_imag
        prod_imag = back_imag * kernel_real - back_real * kernel_imag
        inner_real, inner_imag = transform(stack(prod_real, prod_imag), inverse)
        wave_real, wave_imag = saved[layer]
        pieces[layer] = jnp.stack(
            [wave_real * inner_real + wave_imag * inner_imag,
             wave_real * inner_imag - wave_imag * inner_real],
            axis=0,
        )
        if layer > 0:
            layer_real = layers[layer][0]
            layer_imag = layers[layer][1]
            grad_real = layer_real * inner_real + layer_imag * inner_imag
            grad_imag = layer_real * inner_imag - layer_imag * inner_real
    piece = jnp.take(jnp.stack(pieces, axis=0), cut_index, axis=0)

    padded = jnp.concatenate([piece, jnp.zeros_like(piece)], axis=1)
    spill = lax.dynamic_slice(padded, (zero, rows - row, zero), (2, width, width))
    arrived = jnp.stack([shifted(spill[0], "tile", 1), shifted(spill[1], "tile", 1)], axis=0)

    own = jnp.pad(piece, ((0, 0), (rows, rows), (columns, columns)))
    own = lax.dynamic_slice(own, (zero, rows - row, columns - column), (2, rows, columns))
    above = jnp.pad(arrived, ((0, 0), (0, rows), (columns, columns)))
    above = lax.dynamic_slice(above, (zero, zero, columns - column_above), (2, rows, columns))
    result = own + above
    return result[None]


def solution(mesh):
    placed = (P("cuts", None, "tile", None), P(), P(), P("tile"), P("tile"), P("tile", None, None))
    return jax.shard_map(
        per_device,
        mesh=mesh,
        in_specs=placed,
        out_specs=P("cuts", None, "tile", None),
        check_vma=False,
    )
```

```python
import jax
import jax.numpy as jnp
from jax import lax
from jax.experimental import pallas as pl
from jax.experimental.pallas import tpu as pltpu
from jax.sharding import PartitionSpec as P


def shifted(value, axis, by):
    devices = lax.axis_size(axis)
    pairs = [(i, i + by) for i in range(devices) if 0 <= i + by < devices]
    return lax.ppermute(value, axis, pairs)


def rotated(value, axis, by):
    devices = lax.axis_size(axis)
    pairs = [(i, (i + by) % devices) for i in range(devices)]
    return lax.ppermute(value, axis, pairs)


def dft_tables(length):
    index = lax.iota(jnp.int32, length)
    product = index[:, None] * index[None, :] % length
    angle = product.astype(jnp.float32) * (2.0 * jnp.pi / length)
    factor = 1.0 / jnp.sqrt(jnp.float32(length))
    return (jnp.cos(angle) * factor, jnp.sin(angle) * factor)


def halves(value):
    scaled = value * jnp.float32(65537.0)
    high = scaled - (scaled - value)
    low = value - high
    return high.astype(jnp.bfloat16), low.astype(jnp.bfloat16)


def stacked_tables(cosines, sines, direction):
    signed = sines * direction
    parts = jnp.stack([cosines, cosines + signed, signed - cosines])
    high, low = halves(parts)
    left = jnp.concatenate([high, high, low], axis=2)
    right = jnp.concatenate([high, low, high], axis=1)
    return left, right


def transform(stacked, tables):
    left, right = tables
    real, imag = stacked
    high, low = halves(jnp.stack([real + imag, imag, real]))
    operand = jnp.concatenate([high, low, high], axis=1)
    terms = jnp.einsum("bij,bjk->bik", left, operand, preferred_element_type=jnp.float32)
    middle_real = terms[0] - terms[1]
    middle_imag = terms[0] + terms[2]
    high, low = halves(jnp.stack([middle_real + middle_imag, middle_imag, middle_real]))
    operand = jnp.concatenate([high, high, low], axis=2)
    terms = jnp.einsum("bij,bjk->bik", operand, right, preferred_element_type=jnp.float32)
    return terms[0] - terms[1], terms[0] + terms[2]


def stack(real_part, imag_part):
    return (real_part, imag_part)


def exchange_kernel(window_ref, layers_ref, send_sem, recv_sem):
    devices = lax.axis_size("cuts")
    me = lax.axis_index("cuts")
    right = lax.rem(me + 1, devices)
    left = lax.rem(me + devices - 1, devices)
    mesh_ids = pl.DeviceIdType.MESH
    barrier = pltpu.get_barrier_semaphore()
    for neighbour in (left, right):
        pl.semaphore_signal(barrier, inc=1, device_id={"cuts": neighbour}, device_id_type=mesh_ids)
    pl.semaphore_wait(barrier, 2)

    def remote(source, target, slot, neighbour):
        return pltpu.make_async_remote_copy(
            src_ref=source,
            dst_ref=target,
            send_sem=send_sem.at[slot],
            recv_sem=recv_sem.at[slot],
            device_id={"cuts": neighbour},
            device_id_type=mesh_ids,
        )

    passed_left = remote(window_ref.at[0], layers_ref.at[me, 0], 0, left)
    passed_right = remote(window_ref.at[1], layers_ref.at[me, 1], 1, right)
    passed_left.start()
    passed_right.start()
    layers_ref[me] = window_ref[...]
    passed_left.wait()
    passed_right.wait()
    far_real = remote(layers_ref.at[right, 0], layers_ref.at[right, 0], 2, left)
    far_imag = remote(layers_ref.at[left, 1], layers_ref.at[left, 1], 3, right)
    far_real.start()
    far_imag.start()
    kept_left = remote(window_ref.at[1], layers_ref.at[me, 1], 4, left)
    kept_right = remote(window_ref.at[0], layers_ref.at[me, 0], 5, right)
    kept_left.start()
    kept_right.start()
    far_real.wait()
    far_imag.wait()
    kept_left.wait()
    kept_right.wait()


def exchange(window, sections):
    shape = jax.ShapeDtypeStruct((sections,) + window.shape, window.dtype)
    vmem = pl.BlockSpec(memory_space=pltpu.VMEM)
    return pl.pallas_call(
        exchange_kernel,
        out_shape=shape,
        in_specs=[vmem],
        out_specs=vmem,
        scratch_shapes=[pltpu.SemaphoreType.DMA((6,)), pltpu.SemaphoreType.DMA((6,))],
        compiler_params=pltpu.CompilerParams(collective_id=0, has_side_effects=True),
    )(window)


def per_device(transmission, probe, prop_phase, row_off, col_off, measured):
    rows = transmission.shape[2]
    columns = transmission.shape[3]
    width = probe.shape[1]
    sections = lax.axis_size("cuts")
    cut_index = lax.axis_index("cuts")
    cosines, sines = dft_tables(width)
    forward = stacked_tables(cosines, sines, -1.0)
    inverse = stacked_tables(cosines, sines, 1.0)
    kernel_real = jnp.cos(prop_phase)
    kernel_imag = jnp.sin(prop_phase)
    zero = jnp.zeros((), jnp.int32)
    row = row_off[0]
    column = col_off[0]
    offsets_above = shifted(jnp.stack([row, column]), "tile", 1)
    row_above = offsets_above[0]
    column_above = offsets_above[1]

    strip = transmission[0]
    lent = lax.dynamic_slice(strip, (zero, zero, column_above), (2, width, width))
    lent = jnp.pad(lent, ((0, 0), (width, 0), (0, 0)))
    lent = lax.dynamic_slice(lent, (zero, row_above, zero), (2, width, width))
    borrowed = shifted(lent, "tile", -1)
    kept = jnp.pad(strip, ((0, 0), (0, width), (0, 0)))
    kept = lax.dynamic_slice(kept, (zero, row, column), (2, width, width))
    window = kept + borrowed

    if sections == 4:
        stacked_layers = exchange(window, sections)
        layers = [stacked_layers[layer] for layer in range(sections)]
    else:
        have = [window] + [rotated(window, "cuts", k) for k in range(1, sections)]
        layers = [
            lax.select_n((cut_index - layer) % sections, *have) for layer in range(sections)
        ]

    wave_real = probe[0]
    wave_imag = probe[1]
    saved = []
    for layer in range(sections):
        saved.append((wave_real, wave_imag))
        layer_real = layers[layer][0]
        layer_imag = layers[layer][1]
        mixed_real = wave_real * layer_real - wave_imag * layer_imag
        mixed_imag = wave_real * layer_imag + wave_imag * layer_real
        freq_real, freq_imag = transform(stack(mixed_real, mixed_imag), forward)
        prod_real = freq_real * kernel_real - freq_imag * kernel_imag
        prod_imag = freq_real * kernel_imag + freq_imag * kernel_real
        if layer < sections - 1:
            wave_real, wave_imag = transform(stack(prod_real, prod_imag), inverse)
    far_real, far_imag = prod_real, prod_imag
    residual = far_real * far_real + far_imag * far_imag - measured[0]
    back_real = residual * far_real
    back_imag = residual * far_imag
    pieces = [None] * sections
    for layer in range(sections - 1, -1, -1):
        if layer < sections - 1:
            back_real, back_imag = transform(stack(grad_real, grad_imag), forward)
        prod_real = back_real * kernel_real + back_imag * kernel_imag
        prod_imag = back_imag * kernel_real - back_real * kernel_imag
        inner_real, inner_imag = transform(stack(prod_real, prod_imag), inverse)
        wave_real, wave_imag = saved[layer]
        pieces[layer] = jnp.stack(
            [wave_real * inner_real + wave_imag * inner_imag,
             wave_real * inner_imag - wave_imag * inner_real],
            axis=0,
        )
        if layer > 0:
            layer_real = layers[layer][0]
            layer_imag = layers[layer][1]
            grad_real = layer_real * inner_real + layer_imag * inner_imag
            grad_imag = layer_real * inner_imag - layer_imag * inner_real
    piece = jnp.take(jnp.stack(pieces, axis=0), cut_index, axis=0)

    padded = jnp.concatenate([piece, jnp.zeros_like(piece)], axis=1)
    spill = lax.dynamic_slice(padded, (zero, rows - row, zero), (2, width, width))
    arrived = shifted(spill, "tile", 1)

    own = jnp.pad(piece, ((0, 0), (rows, rows), (columns, columns)))
    own = lax.dynamic_slice(own, (zero, rows - row, columns - column), (2, rows, columns))
    above = jnp.pad(arrived, ((0, 0), (0, rows), (columns, columns)))
    above = lax.dynamic_slice(above, (zero, zero, columns - column_above), (2, rows, columns))
    result = own + above
    return result[None]


def solution(mesh):
    placed = (P("cuts", None, "tile", None), P(), P(), P("tile"), P("tile"), P("tile", None, None))
    return jax.shard_map(
        per_device,
        mesh=mesh,
        in_specs=placed,
        out_specs=P("cuts", None, "tile", None),
        check_vma=False,
    )
```

```python
import jax
import jax.numpy as jnp
from jax import lax
from jax.experimental import pallas as pl
from jax.experimental.pallas import tpu as pltpu
from jax.sharding import PartitionSpec as P


def shifted(value, axis, by):
    devices = lax.axis_size(axis)
    pairs = [(i, i + by) for i in range(devices) if 0 <= i + by < devices]
    return lax.ppermute(value, axis, pairs)


def rotated(value, axis, by):
    devices = lax.axis_size(axis)
    pairs = [(i, (i + by) % devices) for i in range(devices)]
    return lax.ppermute(value, axis, pairs)


def dft_tables(length):
    index = lax.iota(jnp.int32, length)
    product = index[:, None] * index[None, :] % length
    angle = product.astype(jnp.float32) * (2.0 * jnp.pi / length)
    factor = 1.0 / jnp.sqrt(jnp.float32(length))
    return (jnp.cos(angle) * factor, jnp.sin(angle) * factor)


def halves(value):
    scaled = value * jnp.float32(65537.0)
    high = scaled - (scaled - value)
    low = value - high
    return high.astype(jnp.bfloat16), low.astype(jnp.bfloat16)


def stacked_tables(cosines, sines, direction):
    signed = sines * direction
    parts = jnp.stack([cosines, cosines + signed, signed - cosines])
    high, low = halves(parts)
    left = jnp.concatenate([high, high, low], axis=2)
    right = jnp.concatenate([high, low, high], axis=1)
    return left, right


def transform(stacked, tables):
    left, right = tables
    real, imag = stacked
    high, low = halves(jnp.stack([real + imag, imag, real]))
    operand = jnp.concatenate([high, low, high], axis=1)
    terms = jnp.einsum("bij,bjk->bik", left, operand, preferred_element_type=jnp.float32)
    middle_real = terms[0] - terms[1]
    middle_imag = terms[0] + terms[2]
    high, low = halves(jnp.stack([middle_real + middle_imag, middle_imag, middle_real]))
    operand = jnp.concatenate([high, high, low], axis=2)
    terms = jnp.einsum("bij,bjk->bik", operand, right, preferred_element_type=jnp.float32)
    return terms[0] - terms[1], terms[0] + terms[2]


def stack(real_part, imag_part):
    return (real_part, imag_part)


def exchange_kernel(window_ref, layers_ref, send_sem, recv_sem):
    devices = lax.axis_size("cuts")
    me = lax.axis_index("cuts")
    right = lax.rem(me + 1, devices)
    left = lax.rem(me + devices - 1, devices)
    mesh_ids = pl.DeviceIdType.MESH
    barrier = pltpu.get_barrier_semaphore()
    for neighbour in (left, right):
        pl.semaphore_signal(barrier, inc=1, device_id={"cuts": neighbour}, device_id_type=mesh_ids)
    pl.semaphore_wait(barrier, 2)

    def remote(source, target, slot, neighbour):
        return pltpu.make_async_remote_copy(
            src_ref=source,
            dst_ref=target,
            send_sem=send_sem.at[slot],
            recv_sem=recv_sem.at[slot],
            device_id={"cuts": neighbour},
            device_id_type=mesh_ids,
        )

    passed_left = remote(window_ref.at[0], layers_ref.at[me, 0], 0, left)
    passed_right = remote(window_ref.at[1], layers_ref.at[me, 1], 1, right)
    passed_left.start()
    passed_right.start()
    layers_ref[me] = window_ref[...]
    passed_left.wait()
    passed_right.wait()
    far_real = remote(layers_ref.at[right, 0], layers_ref.at[right, 0], 2, left)
    far_imag = remote(layers_ref.at[left, 1], layers_ref.at[left, 1], 3, right)
    far_real.start()
    far_imag.start()
    kept_left = remote(window_ref.at[1], layers_ref.at[me, 1], 4, left)
    kept_right = remote(window_ref.at[0], layers_ref.at[me, 0], 5, right)
    kept_left.start()
    kept_right.start()
    far_real.wait()
    far_imag.wait()
    kept_left.wait()
    kept_right.wait()


def exchange(window, sections):
    shape = jax.ShapeDtypeStruct((sections,) + window.shape, window.dtype)
    vmem = pl.BlockSpec(memory_space=pltpu.VMEM)
    return pl.pallas_call(
        exchange_kernel,
        out_shape=shape,
        in_specs=[vmem],
        out_specs=vmem,
        scratch_shapes=[pltpu.SemaphoreType.DMA((6,)), pltpu.SemaphoreType.DMA((6,))],
        compiler_params=pltpu.CompilerParams(collective_id=0, has_side_effects=True),
    )(window)


def per_device(transmission, probe, prop_phase, row_off, col_off, measured):
    rows = transmission.shape[2]
    columns = transmission.shape[3]
    width = probe.shape[1]
    sections = lax.axis_size("cuts")
    cut_index = lax.axis_index("cuts")
    cosines, sines = dft_tables(width)
    forward = stacked_tables(cosines, sines, -1.0)
    inverse = stacked_tables(cosines, sines, 1.0)
    kernel_real = jnp.cos(prop_phase)
    kernel_imag = jnp.sin(prop_phase)
    zero = jnp.zeros((), jnp.int32)
    row = row_off[0]
    column = col_off[0]
    offsets_above = shifted(jnp.stack([row, column]), "tile", 1)
    row_above = offsets_above[0]
    column_above = offsets_above[1]

    strip = transmission[0]
    lent = jnp.pad(strip, ((0, 0), (width, 0), (0, 0)))
    lent = lax.dynamic_slice(lent, (zero, row_above, column_above), (2, width, width))
    borrowed = shifted(lent, "tile", -1)
    kept = jnp.pad(strip, ((0, 0), (0, width), (0, 0)))
    kept = lax.dynamic_slice(kept, (zero, row, column), (2, width, width))
    window = kept + borrowed

    if sections == 4:
        stacked_layers = exchange(window, sections)
        layers = [stacked_layers[layer] for layer in range(sections)]
    else:
        have = [window] + [rotated(window, "cuts", k) for k in range(1, sections)]
        layers = [
            lax.select_n((cut_index - layer) % sections, *have) for layer in range(sections)
        ]

    wave_real = probe[0]
    wave_imag = probe[1]
    saved = []
    for layer in range(sections):
        saved.append((wave_real, wave_imag))
        layer_real = layers[layer][0]
        layer_imag = layers[layer][1]
        mixed_real = wave_real * layer_real - wave_imag * layer_imag
        mixed_imag = wave_real * layer_imag + wave_imag * layer_real
        freq_real, freq_imag = transform(stack(mixed_real, mixed_imag), forward)
        prod_real = freq_real * kernel_real - freq_imag * kernel_imag
        prod_imag = freq_real * kernel_imag + freq_imag * kernel_real
        if layer < sections - 1:
            wave_real, wave_imag = transform(stack(prod_real, prod_imag), inverse)
    far_real, far_imag = prod_real, prod_imag
    residual = far_real * far_real + far_imag * far_imag - measured[0]
    back_real = residual * far_real
    back_imag = residual * far_imag
    pieces = [None] * sections
    for layer in range(sections - 1, -1, -1):
        if layer < sections - 1:
            back_real, back_imag = transform(stack(grad_real, grad_imag), forward)
        prod_real = back_real * kernel_real + back_imag * kernel_imag
        prod_imag = back_imag * kernel_real - back_real * kernel_imag
        inner_real, inner_imag = transform(stack(prod_real, prod_imag), inverse)
        wave_real, wave_imag = saved[layer]
        pieces[layer] = jnp.stack(
            [wave_real * inner_real + wave_imag * inner_imag,
             wave_real * inner_imag - wave_imag * inner_real],
            axis=0,
        )
        if layer > 0:
            layer_real = layers[layer][0]
            layer_imag = layers[layer][1]
            grad_real = layer_real * inner_real + layer_imag * inner_imag
            grad_imag = layer_real * inner_imag - layer_imag * inner_real
    piece = jnp.take(jnp.stack(pieces, axis=0), cut_index, axis=0)

    padded = jnp.concatenate([piece, jnp.zeros_like(piece)], axis=1)
    spill = lax.dynamic_slice(padded, (zero, rows - row, zero), (2, width, width))
    arrived = shifted(spill, "tile", 1)

    own = jnp.pad(piece, ((0, 0), (rows, rows), (columns, columns)))
    own = lax.dynamic_slice(own, (zero, rows - row, columns - column), (2, rows, columns))
    above = jnp.pad(arrived, ((0, 0), (0, rows), (columns, columns)))
    above = lax.dynamic_slice(above, (zero, zero, columns - column_above), (2, rows, columns))
    result = own + above
    return result[None]


def solution(mesh):
    placed = (P("cuts", None, "tile", None), P(), P(), P("tile"), P("tile"), P("tile", None, None))
    return jax.shard_map(
        per_device,
        mesh=mesh,
        in_specs=placed,
        out_specs=P("cuts", None, "tile", None),
        check_vma=False,
    )
```

```python
import jax
import jax.numpy as jnp
from jax import lax
from jax.experimental import pallas as pl
from jax.experimental.pallas import tpu as pltpu
from jax.sharding import PartitionSpec as P


def shifted(value, axis, by):
    devices = lax.axis_size(axis)
    pairs = [(i, i + by) for i in range(devices) if 0 <= i + by < devices]
    return lax.ppermute(value, axis, pairs)


def rotated(value, axis, by):
    devices = lax.axis_size(axis)
    pairs = [(i, (i + by) % devices) for i in range(devices)]
    return lax.ppermute(value, axis, pairs)


def dft_tables(length):
    index = lax.iota(jnp.int32, length)
    product = index[:, None] * index[None, :] % length
    angle = product.astype(jnp.float32) * (2.0 * jnp.pi / length)
    factor = 1.0 / jnp.sqrt(jnp.float32(length))
    return (jnp.cos(angle) * factor, jnp.sin(angle) * factor)


def halves(value):
    scaled = value * jnp.float32(65537.0)
    high = scaled - (scaled - value)
    low = value - high
    return high.astype(jnp.bfloat16), low.astype(jnp.bfloat16)


def stacked_tables(cosines, sines, direction):
    signed = sines * direction
    parts = jnp.stack([cosines, cosines + signed, signed - cosines])
    high, low = halves(parts)
    left = jnp.concatenate([high, high, low], axis=2)
    right = jnp.concatenate([high, low, high], axis=1)
    return left, right


def transform(stacked, tables):
    left, right = tables
    real, imag = stacked
    high, low = halves(jnp.stack([real + imag, imag, real]))
    operand = jnp.concatenate([high, low, high], axis=1)
    terms = jnp.einsum("bij,bjk->bik", left, operand, preferred_element_type=jnp.float32)
    middle_real = terms[0] - terms[1]
    middle_imag = terms[0] + terms[2]
    high, low = halves(jnp.stack([middle_real + middle_imag, middle_imag, middle_real]))
    operand = jnp.concatenate([high, high, low], axis=2)
    terms = jnp.einsum("bij,bjk->bik", operand, right, preferred_element_type=jnp.float32)
    return terms[0] - terms[1], terms[0] + terms[2]


def stack(real_part, imag_part):
    return (real_part, imag_part)


def exchange_kernel(window_ref, layers_ref, send_sem, recv_sem):
    devices = lax.axis_size("cuts")
    me = lax.axis_index("cuts")
    right = lax.rem(me + 1, devices)
    left = lax.rem(me + devices - 1, devices)
    mesh_ids = pl.DeviceIdType.MESH
    barrier = pltpu.get_barrier_semaphore()
    for neighbour in (left, right):
        pl.semaphore_signal(barrier, inc=1, device_id={"cuts": neighbour}, device_id_type=mesh_ids)
    pl.semaphore_wait(barrier, 2)

    def remote(source, target, slot, neighbour):
        return pltpu.make_async_remote_copy(
            src_ref=source,
            dst_ref=target,
            send_sem=send_sem.at[slot],
            recv_sem=recv_sem.at[slot],
            device_id={"cuts": neighbour},
            device_id_type=mesh_ids,
        )

    passed_left = remote(window_ref.at[0], layers_ref.at[me, 0], 0, left)
    passed_right = remote(window_ref.at[1], layers_ref.at[me, 1], 1, right)
    passed_left.start()
    passed_right.start()
    layers_ref[me] = window_ref[...]
    passed_left.wait()
    passed_right.wait()
    far_real = remote(layers_ref.at[right, 0], layers_ref.at[right, 0], 2, left)
    far_imag = remote(layers_ref.at[left, 1], layers_ref.at[left, 1], 3, right)
    far_real.start()
    far_imag.start()
    kept_left = remote(window_ref.at[1], layers_ref.at[me, 1], 4, left)
    kept_right = remote(window_ref.at[0], layers_ref.at[me, 0], 5, right)
    kept_left.start()
    kept_right.start()
    far_real.wait()
    far_imag.wait()
    kept_left.wait()
    kept_right.wait()


def exchange(window, sections):
    shape = jax.ShapeDtypeStruct((sections,) + window.shape, window.dtype)
    vmem = pl.BlockSpec(memory_space=pltpu.VMEM)
    return pl.pallas_call(
        exchange_kernel,
        out_shape=shape,
        in_specs=[vmem],
        out_specs=vmem,
        scratch_shapes=[pltpu.SemaphoreType.DMA((6,)), pltpu.SemaphoreType.DMA((6,))],
        compiler_params=pltpu.CompilerParams(collective_id=0, has_side_effects=True),
    )(window)


def per_device(transmission, probe, prop_phase, row_off, col_off, measured):
    rows = transmission.shape[2]
    columns = transmission.shape[3]
    width = probe.shape[1]
    sections = lax.axis_size("cuts")
    cut_index = lax.axis_index("cuts")
    cosines, sines = dft_tables(width)
    forward = stacked_tables(cosines, sines, -1.0)
    inverse = stacked_tables(cosines, sines, 1.0)
    kernel_real = jnp.cos(prop_phase)
    kernel_imag = jnp.sin(prop_phase)
    zero = jnp.zeros((), jnp.int32)
    row = row_off[0]
    column = col_off[0]
    offsets_above = shifted(jnp.stack([row, column]), "tile", 1)
    row_above = offsets_above[0]
    column_above = offsets_above[1]

    strip = transmission[0]
    pick_rows = (
        lax.broadcasted_iota(jnp.int32, (width, rows), 1)
        == lax.broadcasted_iota(jnp.int32, (width, rows), 0) + (row_above - width)
    ).astype(jnp.float32)
    pick_columns = (
        lax.broadcasted_iota(jnp.int32, (columns, width), 0)
        == lax.broadcasted_iota(jnp.int32, (columns, width), 1) + column_above
    ).astype(jnp.float32)
    lent = jnp.einsum("rn,cnk->crk", pick_rows, strip, precision=lax.Precision.HIGHEST)
    lent = jnp.einsum("crn,nk->crk", lent, pick_columns, precision=lax.Precision.HIGHEST)
    borrowed = shifted(lent, "tile", -1)
    kept = jnp.pad(strip, ((0, 0), (0, width), (0, 0)))
    kept = lax.dynamic_slice(kept, (zero, row, column), (2, width, width))
    window = kept + borrowed

    if sections == 4:
        stacked_layers = exchange(window, sections)
        layers = [stacked_layers[layer] for layer in range(sections)]
    else:
        have = [window] + [rotated(window, "cuts", k) for k in range(1, sections)]
        layers = [
            lax.select_n((cut_index - layer) % sections, *have) for layer in range(sections)
        ]

    wave_real = probe[0]
    wave_imag = probe[1]
    saved = []
    for layer in range(sections):
        saved.append((wave_real, wave_imag))
        layer_real = layers[layer][0]
        layer_imag = layers[layer][1]
        mixed_real = wave_real * layer_real - wave_imag * layer_imag
        mixed_imag = wave_real * layer_imag + wave_imag * layer_real
        freq_real, freq_imag = transform(stack(mixed_real, mixed_imag), forward)
        prod_real = freq_real * kernel_real - freq_imag * kernel_imag
        prod_imag = freq_real * kernel_imag + freq_imag * kernel_real
        if layer < sections - 1:
            wave_real, wave_imag = transform(stack(prod_real, prod_imag), inverse)
    far_real, far_imag = prod_real, prod_imag
    residual = far_real * far_real + far_imag * far_imag - measured[0]
    back_real = residual * far_real
    back_imag = residual * far_imag
    pieces = [None] * sections
    for layer in range(sections - 1, -1, -1):
        if layer < sections - 1:
            back_real, back_imag = transform(stack(grad_real, grad_imag), forward)
        prod_real = back_real * kernel_real + back_imag * kernel_imag
        prod_imag = back_imag * kernel_real - back_real * kernel_imag
        inner_real, inner_imag = transform(stack(prod_real, prod_imag), inverse)
        wave_real, wave_imag = saved[layer]
        pieces[layer] = jnp.stack(
            [wave_real * inner_real + wave_imag * inner_imag,
             wave_real * inner_imag - wave_imag * inner_real],
            axis=0,
        )
        if layer > 0:
            layer_real = layers[layer][0]
            layer_imag = layers[layer][1]
            grad_real = layer_real * inner_real + layer_imag * inner_imag
            grad_imag = layer_real * inner_imag - layer_imag * inner_real
    piece = jnp.take(jnp.stack(pieces, axis=0), cut_index, axis=0)

    padded = jnp.concatenate([piece, jnp.zeros_like(piece)], axis=1)
    spill = lax.dynamic_slice(padded, (zero, rows - row, zero), (2, width, width))
    arrived = shifted(spill, "tile", 1)

    own = jnp.pad(piece, ((0, 0), (rows, rows), (columns, columns)))
    own = lax.dynamic_slice(own, (zero, rows - row, columns - column), (2, rows, columns))
    above = jnp.pad(arrived, ((0, 0), (0, rows), (columns, columns)))
    above = lax.dynamic_slice(above, (zero, zero, columns - column_above), (2, rows, columns))
    result = own + above
    return result[None]


def solution(mesh):
    placed = (P("cuts", None, "tile", None), P(), P(), P("tile"), P("tile"), P("tile", None, None))
    return jax.shard_map(
        per_device,
        mesh=mesh,
        in_specs=placed,
        out_specs=P("cuts", None, "tile", None),
        check_vma=False,
    )
```
